32 devices in a mesh: groups: 2 (over y), seq: 4 (over z), mp: 2 (over x), enc: 2 (over core).
Axes of the slice: x: 2, y: 2, z: 4, core: 2. Of those that a mesh axis runs over, the one named last changes fastest.
Arguments:
- tokens: bfloat16 [4096, 4096], P(('groups', 'seq'), ('mp', 'enc')), parts along dimension 0, may hold values from -6 to 6
- nbr_feats: bfloat16 [192, 128, 4096], P(('groups', 'seq'), None, ('mp', 'enc')), parts along dimension 0, may hold values from -6 to 6
- counts: int32 [8], P('groups'), parts along dimension 0, may hold values from 8 to 24, as said below
- slot_target: int32 [192], P(('groups', 'seq')), parts along dimension 0, may hold values from 0 to 63, as said below
- w_query: bfloat16 [4096, 512], P(None, ('mp', 'enc')), may hold values from -32 to 32
- w_keyval: bfloat16 [4096, 512], P(None, ('mp', 'enc')), may hold values from -1 to 1
Outputs:
- attended: bfloat16 [4096, 512], P(('groups', 'seq'), ('mp', 'enc')), parts along dimension 0
The draws below stay inside these ranges and needn't reach their ends.
There are 2 independent parts, one for each index of `groups`. The reference program is written for one: setup_inputs(seed, part) draws one part's arguments, and reference() takes and returns one part's arrays. A program takes and returns all parts, laid end to end along the dimension named above; an argument that names none is the same for every part. Nothing has to cross between parts.
Inputs may be any that keep to these rules, and one draw needn't show every extreme that they name: Each seq index's live slots are its first counts slots; the counts sum to 64. `slot_target`: A live slot holds neighbour o * 16 + l of the spans of seq index o; every neighbour is held by exactly one live slot; the live slots of one seq index hold at most 8 neighbours of any one seq index; dead slots hold arbitrary values of the range.
All inputs are finite; a program needn't handle non-finite values.
Results may differ from the reference program's by a relative error of at most 0.003.
The reference program's roundings to bfloat16 on the way count: a program that leaves them out, or rounds other values in their place, can miss the bound.
Values may be sent and summed in bfloat16 or wider, within the bound.
A program may use at most 128 MiB of HBM per device.

```python
import math
import jax
import jax.numpy as jnp
from jax import lax

D = 4096
HD = 128
SPAN = 64
NBR = 2
RLEN = 128
KV_HEADS = 2
Q_HEADS = 4
NB_SEQ = 16
ENC_CAP = 24
TOKENS = 2048
NB_ALL = 64
SLOTS = 96
N_SEQ = 4


def shuffled_positions(sub_key):
    return jax.random.permutation(sub_key, NB_SEQ)


def routing_tables(key):
    base_key = jax.random.fold_in(key, 17)
    keys_list = jax.random.split(base_key, 7)
    half_share = NB_SEQ // 2
    pair_cap = max(2, 2 * NB_SEQ // N_SEQ)
    rank_order = jax.random.permutation(keys_list[0], N_SEQ)
    shifts = jax.random.randint(keys_list[1], (N_SEQ // 2,), 0, half_share + 1)
    forced = jax.random.randint(keys_list[2], (), 0, N_SEQ // 2)
    shifts = jnp.where(jnp.arange(N_SEQ // 2) == forced, half_share, shifts)
    paired = jnp.stack([NB_SEQ + shifts, NB_SEQ - shifts], axis=1).reshape(N_SEQ)
    counts = jnp.zeros((N_SEQ,), jnp.int32).at[rank_order].set(paired.astype(jnp.int32))
    starts = jnp.cumsum(counts) - counts
    owner_order = jax.random.permutation(keys_list[3], N_SEQ)
    local_keys = jax.random.split(keys_list[4], N_SEQ)
    local_order = jax.vmap(shuffled_positions)(local_keys)
    places = jnp.arange(NB_SEQ * N_SEQ)
    owners = owner_order[places // pair_cap % N_SEQ]
    occurrence = places // (pair_cap * N_SEQ) * pair_cap + places % pair_cap
    targets = owners * NB_SEQ + local_order[owners, occurrence]
    slot_ids = jnp.arange(ENC_CAP)
    live_slots = slot_ids[None, :] < counts[:, None]
    noise_draw = jax.random.randint(keys_list[5], (N_SEQ, ENC_CAP), 0, 1 << 20)
    scores = jnp.where(live_slots, noise_draw * ENC_CAP + slot_ids[None, :], (1 << 26) + slot_ids[None, :])
    slot_order = jnp.argsort(scores, axis=1)
    picked = jnp.clip(starts[:, None] + slot_order, 0, NB_SEQ * N_SEQ - 1)
    filler = jax.random.randint(keys_list[6], (N_SEQ, ENC_CAP), 0, NB_SEQ * N_SEQ)
    slot_target = jnp.where(live_slots, targets[picked], filler)
    return (counts, slot_target.reshape(N_SEQ * ENC_CAP).astype(jnp.int32))


def draw_counts(key, part):
    return routing_tables(key)[0]


def draw_slot_target(key, part):
    return routing_tables(key)[1]


def weight_base(key):
    return jax.random.normal(jax.random.fold_in(key, 101), (D, KV_HEADS, HD), jnp.float32)


def draw_w_keyval(key, part):
    base = weight_base(key)
    others = jax.random.normal(jax.random.fold_in(key, 202), (D, KV_HEADS, HD), jnp.float32)
    stacked = jnp.stack([base, others], axis=2) / math.sqrt(D)
    stacked = jnp.clip(stacked, -1.0, 1.0)
    return stacked.reshape(D, KV_HEADS * 2 * HD).astype(jnp.bfloat16)


def draw_w_query(key, part):
    noise_draw = jax.random.normal(jax.random.fold_in(key, 303), (D, KV_HEADS, 2, HD), jnp.float32)
    mixed = noise_draw
    scaled = jnp.clip(mixed / math.sqrt(D), -32.0, 32.0)
    return scaled.reshape(D, KV_HEADS * 2 * HD).astype(jnp.bfloat16)


def block_scale(rng, dims, shards, least, high):
    def one(axis_at, shards_of):
        steps = jax.random.uniform(jax.random.fold_in(jax.random.fold_in(rng, 6), axis_at), (shards_of,), jnp.float32, least / len(shards), high / len(shards))
        return jnp.repeat(jnp.exp(steps), dims[axis_at] // shards_of).reshape((-1,) + (1,) * (len(dims) - axis_at - 1))

    level = one(*shards[0])
    for cut in shards[1:]:
        level = level * one(*cut)
    return level


def scatter_about(own_key, shape, width, limit, shards=(), kind=jnp.bfloat16):
    values = jax.random.normal(own_key, shape, jnp.float32) * width
    if len(shards) > 0:
        values = block_scale(own_key, shape, shards, -0.22, 0.18) * values
    return jnp.clip(values, min=-limit, max=limit).astype(kind)


def setup_inputs(seed: int = 0, part: int = 0) -> dict:
    arg_keys = jax.random.split(jax.random.key(seed), 7)
    own_keys = jax.random.split(jax.random.fold_in(arg_keys[6], part), 7)
    tokens = scatter_about(own_keys[0], (TOKENS, D), 1.0, 6.0, ((0, 4), (1, 4)))
    nbr_feats = scatter_about(own_keys[1], (SLOTS, RLEN, D), 1.0, 6.0, ((0, 4), (2, 4)))
    counts = draw_counts(jax.random.fold_in(jax.random.fold_in(arg_keys[6], part), 71), part)
    slot_target = draw_slot_target(jax.random.fold_in(jax.random.fold_in(arg_keys[6], part), 71), part)
    w_query = draw_w_query(jax.random.fold_in(arg_keys[6], 71), part)
    w_keyval = draw_w_keyval(jax.random.fold_in(arg_keys[6], 71), part)
    return {"tokens": tokens, "nbr_feats": nbr_feats, "counts": counts, "slot_target": slot_target, "w_query": w_query, "w_keyval": w_keyval}


epsilon = 1e-05

def settle(value):
    return lax.optimization_barrier(value.astype(jnp.bfloat16)).astype(jnp.float32)

def reference(tokens, nbr_feats, counts, slot_target, w_query, w_keyval):
    slot_ids = jnp.arange(SLOTS, dtype=jnp.int32)
    slot_owner = (slot_ids // ENC_CAP).astype(jnp.int32)
    live_slots = slot_ids % ENC_CAP < counts[slot_owner]
    where_to = jnp.where(live_slots, slot_target, NB_ALL).astype(jnp.int32)
    source = jnp.zeros((NB_ALL,), jnp.int32).at[where_to].set(slot_ids, mode='drop')

    def encode_one(slot):
        features = lax.dynamic_index_in_dim(nbr_feats, slot, 0, keepdims=False)
        product = jnp.dot(features, w_keyval, preferred_element_type=jnp.float32)
        widened = features.astype(jnp.float32)
        scale_rows = lax.rsqrt(lax.optimization_barrier(jnp.sum(widened * widened, axis=1)) / D + epsilon)
        return (product * scale_rows[:, None]).astype(jnp.bfloat16)
    encoded = lax.map(encode_one, source)
    product = jnp.dot(tokens, w_query, preferred_element_type=jnp.float32)
    widened = tokens.astype(jnp.float32)
    scale_rows = lax.rsqrt(lax.optimization_barrier(jnp.sum(widened * widened, axis=1)) / D + epsilon) * HD ** (-0.5)
    query = settle(product * scale_rows[:, None])
    spans = TOKENS // SPAN
    query = query.reshape(spans, SPAN, KV_HEADS, 2, HD)
    pairs = encoded.reshape(spans, NBR, RLEN, KV_HEADS, 2, HD)
    key_rows = pairs[:, :, :, :, 0, :].reshape(spans, NBR * RLEN, KV_HEADS, HD)
    value_rows = pairs[:, :, :, :, 1, :].reshape(spans, NBR * RLEN, KV_HEADS, HD)
    zero_block = jnp.zeros((1, NBR * RLEN, KV_HEADS, HD), jnp.bfloat16)
    context_keys = jnp.concatenate([zero_block, key_rows[:-1]], axis=0).astype(jnp.float32)
    context_values = jnp.concatenate([zero_block, value_rows[:-1]], axis=0).astype(jnp.float32)
    scores = jnp.einsum('cqhgd,ckhd->cqhgk', query, context_keys)
    weights = settle(jax.nn.softmax(scores, axis=-1))
    attended = jnp.einsum('cqhgk,ckhd->cqhgd', weights, context_values)
    return attended.astype(jnp.bfloat16).reshape(TOKENS, Q_HEADS * HD)
```

```python
import functools
import jax
import jax.numpy as jnp
from jax import lax
from jax.experimental import pallas as pl
from jax.experimental.pallas import tpu as pltpu
from jax.sharding import PartitionSpec as P

D = 4096
SPAN = 64
NBR = 2
RLEN = 128
CH_SEQ = 8
NB_SEQ = 16
ENC_CAP = 24


epsilon = 1e-05


def partner_2(block, axis, stride):
    count = lax.axis_size(axis)
    route = []
    for low in range(count):
        high = low | 1 << stride
        if high != low and high < count:
            route += [(low, high), (high, low)]
    return lax.ppermute(block, axis, route)


def passed_along(block, axis, distance):
    devices = range(lax.axis_size(axis))
    route = [(i - distance, i) for i in devices if i - distance in devices]
    return lax.ppermute(block, axis, route)


def project_fold(weight, piece):
    width = piece.shape[-1]
    flat_rows = piece.reshape(-1, width)
    mine = lax.all_to_all(weight, ("mp", "enc"), split_axis=0, concat_axis=1, tiled=True)
    partial = jnp.dot(flat_rows, mine, preferred_element_type=jnp.float32)
    running = lax.psum_scatter(partial, ("mp", "enc"), scatter_dimension=1, tiled=True)
    widened = flat_rows.astype(jnp.float32)
    squares = lax.psum(jnp.sum(widened * widened, axis=1), ("mp", "enc"))
    return (running, squares)


def normalized(carry, factor):
    running, squares = carry
    scale_rows = lax.rsqrt(squares / D + epsilon) * factor
    return (running * scale_rows[:, None]).astype(jnp.bfloat16)


def routing_plan(slot_target, counts, pair_cap):
    seq_count = counts.shape[0]
    seq_here = lax.axis_index("seq")
    live_count = jnp.sum(jnp.where(jnp.arange(seq_count) == seq_here, counts, 0))
    slot_ids = jnp.arange(ENC_CAP)
    live_slots = slot_ids < live_count
    owner_of = slot_target // NB_SEQ
    position = slot_target % NB_SEQ
    same_owner = (
        (owner_of[:, None] == owner_of[None, :])
        & live_slots[None, :]
        & (slot_ids[None, :] < slot_ids[:, None])
    )
    rank_within = jnp.sum(same_owner.astype(jnp.int32), axis=1)
    target_slot = owner_of * pair_cap + rank_within
    buffer_ids = jnp.arange(seq_count * pair_cap)
    chosen = (buffer_ids[:, None] == target_slot[None, :]) & live_slots[None, :]
    sent_ids = jnp.sum(jnp.where(chosen, position[None, :] + 1, 0), axis=1) - 1
    return (chosen, sent_ids.reshape(seq_count, pair_cap))


def pack_rows(chosen, payload, seq_count, pair_cap):
    packed = jnp.dot(chosen.astype(jnp.bfloat16), payload, preferred_element_type=jnp.float32)
    return packed.astype(jnp.bfloat16).reshape(seq_count, pair_cap, payload.shape[1])


def place_rows(received, received_ids):
    flat_rows = received.reshape(-1, received.shape[-1])
    picker = received_ids.reshape(1, -1) == jnp.arange(NB_SEQ)[:, None]
    placed = jnp.dot(picker.astype(jnp.bfloat16), flat_rows, preferred_element_type=jnp.float32)
    return placed.astype(jnp.bfloat16)


def local(tokens, nbr_feats, counts, slot_target, w_query, w_keyval):
    seq_count = lax.axis_size("seq")
    pair_cap = max(2, 2 * NB_SEQ // seq_count)
    head_size = w_keyval.shape[1]
    chosen, sent_ids = routing_plan(slot_target, counts, pair_cap)
    folded = project_fold(w_keyval, nbr_feats)
    encoded = normalized(folded, 1.0).reshape(ENC_CAP, RLEN * head_size)
    packed = pack_rows(chosen, encoded, seq_count, pair_cap)
    received, received_ids = (
        lax.all_to_all(packed, "seq", split_axis=0, concat_axis=0, tiled=True),
        lax.all_to_all(sent_ids, "seq", split_axis=0, concat_axis=0, tiled=True),
    )
    own_half = place_rows(received, received_ids).reshape(NB_SEQ, RLEN, head_size)
    partner = partner_2(own_half, "enc", 0)
    first_lane = lax.axis_index("enc") == 0
    key_rows = jnp.where(first_lane, own_half, partner).reshape(CH_SEQ, NBR * RLEN, head_size)
    value_rows = jnp.where(first_lane, partner, own_half).reshape(CH_SEQ, NBR * RLEN, head_size)
    prior_keys, prior_values = passed_along((key_rows[-1], value_rows[-1]), "seq", 1)
    context_keys = jnp.concatenate([prior_keys[None], key_rows[:-1]], axis=0)
    context_values = jnp.concatenate([prior_values[None], value_rows[:-1]], axis=0)
    folded_tokens = project_fold(w_query, tokens)
    queries = normalized(folded_tokens, head_size ** (-0.5)).reshape(CH_SEQ, SPAN, head_size)
    scores = jnp.einsum("cqd,ckd->cqk", queries, context_keys, preferred_element_type=jnp.float32)
    weights = jax.nn.softmax(scores, axis=-1).astype(jnp.bfloat16)
    attended = jnp.einsum(
        "cqk,ckd->cqd", weights, context_values, preferred_element_type=jnp.float32
    )
    return attended.astype(jnp.bfloat16).reshape(CH_SEQ * SPAN, head_size)


CHUNKS = 4
CROWS = RLEN // 2 // CHUNKS
CFLAT = ENC_CAP * CROWS
LINES = CFLAT // 128
TOP = 8388600.0


def fused(
    S, cap, trow, cnt, feats, tokens, wq, wkv, out,
    xb, tb, wown, wo, woq, sown, psend, precv, town, tsend, trecv, ss, st, str_,
    enc, zs, zr, zl, ctx, qb, qs, tab, tabr, pidx_v, lidx_v, pidx, lidx,
    lsem, send, recv,
):
    f32, i32 = jnp.float32, jnp.int32
    g, r, m, e = (lax.axis_index(a) for a in ("groups", "seq", "mp", "enc"))
    pg, pm, pe = 1 - g, 1 - m, 1 - e
    p = lax.rem(r, 2)
    first = e == p
    K = feats.shape[2]
    half = tokens.shape[0] // 2
    C = CHUNKS
    Q = K // 4
    partner, across, beside = {"enc": pe}, {"mp": pm}, {"groups": pg}
    paired = {"seq": r + 1 - 2 * p}

    ids = {}
    total = 0
    for name, count in SEMAPHORES(S):
        ids[name] = total
        total += count

    def rc(src, dst, name, at, device):
        i = ids[name] + at
        return pltpu.make_async_remote_copy(
            src_ref=src, dst_ref=dst, send_sem=send.at[i], recv_sem=recv.at[i],
            device_id=device, device_id_type=pl.DeviceIdType.MESH,
        )

    def landed(dst, name, at, device):
        rc(dst, dst, name, at, device).wait_recv()

    def lanes(index):
        return pl.ds(pl.multiple_of(index * 128, 128), 128)

    def rows(start, size):
        return pl.ds(pl.multiple_of(start, 16), size)

    def zdev(d):
        return {"seq": lax.rem(r + d, S)}

    done = []

    def begin(copy):
        copy.start()
        done.append(copy)

    barrier = pltpu.get_barrier_semaphore()
    for device in [across, beside, partner] + [zdev(d) for d in range(1, S)]:
        pl.semaphore_signal(barrier, inc=1, device_id=device, device_id_type=pl.DeviceIdType.MESH)

    def krow(i):
        return rows((K * g if i < 4 else K * pg) + i % 4 * Q, Q)

    def kx(i):
        source = wkv.at[rows(2 * K * pm + K * g + i * Q, Q), :]
        return rc(source, wo.at[e, krow(i)], "kx", i, across)

    def kstep(name, i, device):
        return rc(wo.at[e, krow(i)], wo.at[e, krow(i)], name, i, device)

    def ky(i):
        return kstep("ky", i, beside)

    def kz(i):
        return kstep("kz", i, paired)

    def ke(i):
        return kstep("ke", i, partner)

    def from_across(i):
        landed(wo.at[e, krow(i)], "kx", i, across)
        ky(i).start()
        ke(i).start()
        kz(i).start()

    def from_beside(i):
        landed(wo.at[e, krow(4 + i)], "ky", i, beside)
        ke(4 + i).start()
        kz(4 + i).start()

    def from_paired(i):
        landed(wo.at[e, krow(i)], "kz", i, paired)
        ke(i).start()

    def from_partner():
        for i in range(8):
            landed(wo.at[pe, krow(i)], "ke", i, partner)

    def qpiece(part, i, side):
        return woq.at[rows(part * K + i * Q, Q), lanes(side)]

    def qx(i):
        source = wq.at[rows(2 * K * pm + K * g + i * Q, Q), :]
        return rc(source, qpiece(g, i, e), "wx", i, across)

    weights = (wkv, wq)

    def weight_local(k):
        source = weights[k].at[rows(2 * K * m, 2 * K), :]
        return pltpu.make_async_copy(source, wown.at[k, :, lanes(e)], lsem.at[C + k])

    def weight_sent(k):
        source = weights[k].at[rows(2 * K * m, 2 * K), :]
        return rc(source, wown.at[k, :, lanes(e)], "wo", k, partner)

    def own_chunk(c):
        return pltpu.make_async_copy(
            feats.at[:, rows(CROWS * C * e + CROWS * c, CROWS), :], xb.at[e, c], lsem.at[c]
        )

    def sent_chunk(c):
        return rc(
            feats.at[:, rows(CROWS * C * pe + CROWS * c, CROWS), :], xb.at[e, c], "x", c, partner
        )

    local_kv = weight_local(0)
    local_kv.start()
    for c in range(C):
        own_chunk(c).start()
    local_q = weight_local(1)
    local_q.start()
    local_t = pltpu.make_async_copy(tokens.at[rows(half * e, half), :], tb.at[e], lsem.at[C + 2])
    local_t.start()

    t_row = trow[...]
    iota = lambda shape, axis: lax.broadcasted_iota(jnp.int32, shape, axis)
    E = ENC_CAP
    t_col = jnp.sum(jnp.where(iota((E, E), 0) == iota((E, E), 1), t_row, 0), axis=1, keepdims=True)
    live = jnp.sum(jnp.where(iota((1, S), 1) == r, cnt[...], 0), axis=1, keepdims=True)
    same = (
        ((t_col >> 4) == (t_row >> 4)) & (iota((E, E), 1) < live) & (iota((E, E), 1) < iota((E, E), 0))
    )
    rank = jnp.sum(jnp.where(same, 1, 0), axis=1, keepdims=True)
    at_lane = iota((E, 128), 1)
    slot = iota((E, 128), 0)
    is_live = slot < live
    wanted = ((t_col >> 4) * cap + rank == at_lane) & is_live
    source_row = jnp.sum(jnp.where(wanted, slot, 0), axis=0, keepdims=True)
    held = (t_col == at_lane) & is_live
    place_row = jnp.sum(jnp.where(held, r * cap + rank, 0), axis=0, keepdims=True)
    pidx_v[...] = jnp.broadcast_to(source_row, (8, 128))
    tab[...] = jnp.broadcast_to(place_row, (8, 128))
    pack_copy = pltpu.make_async_copy(pidx_v, pidx, lsem.at[C + 3])
    pack_copy.start()
    tabr[0] = tab[...]
    ss[...] = jnp.zeros_like(ss)
    st[...] = jnp.zeros_like(st)

    @pl.when(r == 0)
    def _():
        ctx[:, 0:2] = jnp.zeros((2, 2) + ctx.shape[2:], ctx.dtype)

    pl.semaphore_wait(barrier, S + 2)

    @pl.when(first)
    def _():
        for i in range(4):
            kx(i).start()
        for i in range(4):
            qx(i).start()

    begin(weight_sent(0))
    sent_chunk(0).start()
    sent_chunk(1).start()
    for d in range(1, S):
        begin(rc(tab, tabr.at[d], "tab", d, zdev(d)))

    eye = iota((128, 128), 0) == iota((128, 128), 1)

    def as_rows(column):
        blocks = column.reshape(-1, 128, 1)
        return jnp.sum(jnp.where(eye[None], blocks, 0.0), axis=1)

    def as_column(lined):
        blocks = jnp.where(eye[None], lined[:, None, :], 0.0)
        return jnp.sum(blocks, axis=2, keepdims=True).reshape(-1, 1)

    def squares(block):
        wide = block.astype(f32)
        return jnp.sum(wide * wide, axis=1, keepdims=True)

    def product(one, two, weight):
        return jnp.dot(one, weight[:K, :], preferred_element_type=f32) + jnp.dot(
            two, weight[K:, :], preferred_element_type=f32
        )

    def chunk_rows(c):
        return xb[0, c].reshape(CFLAT, K), xb[1, c].reshape(CFLAT, K)

    def own_pass(c):
        own_chunk(c).wait()
        landed(xb.at[pe, c], "x", c, partner)
        one, two = chunk_rows(c)
        ss[c, 0:LINES, :] = as_rows(squares(one) + squares(two))
        sown[c] = product(one, two, wown.at[0])

    def coded(part):
        peak = jnp.maximum(jnp.max(jnp.abs(part), axis=1, keepdims=True), 1e-30)
        whole = jnp.floor(part * (TOP / peak) + 0.5).astype(i32)
        block = part.shape[0] // 4
        last = whole[3 * block :]
        words = [
            (whole[i * block : (i + 1) * block] << 8) | ((last >> (8 * i)) & 255) for i in range(3)
        ]
        return jnp.concatenate(words, axis=0), peak

    def decoded(words, peak):
        block = words.shape[0] // 3
        parts = [words[i * block : (i + 1) * block] for i in range(3)]
        last = ((parts[2] << 24) >> 8) | ((parts[1] & 255) << 8) | (parts[0] & 255)
        whole = jnp.concatenate([word >> 8 for word in parts] + [last], axis=0)
        return whole.astype(f32) * (peak * (1.0 / TOP))

    def half_of(u):
        return lax.rem(u + p, 2)

    def partial_copy(u):
        return rc(psend.at[u], precv.at[u], "s", u, across)

    def stat_copy(u):
        return rc(st.at[u], str_.at[u], "st", u, across)

    def other_pass(u):
        c = u // 2
        one, two = chunk_rows(c)
        words, peak = coded(product(one, two, wo.at[half_of(u)]))
        st[u, 0:LINES, :] = as_rows(peak)
        st[u, LINES : 2 * LINES, :] = ss[c, 0:LINES, :]
        stat_copy(u).start()
        psend[u] = words
        partial_copy(u).start()

    @pl.when(first)
    def _():
        from_across(0)
        from_across(1)

    local_kv.wait()
    landed(wown.at[0, :, lanes(pe)], "wo", 0, partner)
    own_pass(0)

    @pl.when(first)
    def _():
        from_across(2)
        from_across(3)
        from_beside(0)

    @pl.when(jnp.logical_not(first))
    def _():
        for i in range(4):
            qx(i).start()
        from_paired(0)
        from_paired(1)

    sent_chunk(2).start()
    own_pass(1)

    @pl.when(first)
    def _():
        from_beside(1)
        from_beside(2)
        from_beside(3)

    @pl.when(jnp.logical_not(first))
    def _():
        from_paired(2)
        from_paired(3)
        from_partner()

    sent_chunk(3).start()
    other_pass(0)

    @pl.when(jnp.logical_not(first))
    def _():
        for i in range(4, 8):
            from_paired(i)

    own_pass(2)

    @pl.when(first)
    def _():
        from_partner()

    begin(weight_sent(1))
    begin(rc(tokens.at[rows(half * pe, half), :], tb.at[e], "t", 0, partner))
    other_pass(1)
    own_pass(3)

    def other_two(u, carry):
        other_pass(u)
        return carry

    lax.fori_loop(2, 4, other_two, 0)

    for i in range(4):
        here = qpiece(g, i, e)
        landed(here, "wx", i, across)
        begin(rc(here, here, "wy", i, beside))
        begin(rc(here, here, "wf", i, partner))

    for d in range(1, S):
        landed(tabr.at[d], "tab", d, zdev(d))
    places = tabr[0]
    for d in range(1, S):
        places = places + tabr[d]
    lidx_v[...] = places
    place_copy = pltpu.make_async_copy(lidx_v, lidx, lsem.at[C + 4])
    place_copy.start()
    pack_copy.wait()
    place_copy.wait()

    def z_copy(u, d):
        dst = lax.rem(r + d, S)
        return rc(zs.at[u, dst], zr.at[u // 2, half_of(u), r], "z", u * S + d, zdev(d))

    def z_landed(u, d):
        source = lax.rem(r + S - d, S)
        side = lax.rem(u + lax.rem(source, 2), 2)
        landed(zr.at[u // 2, side, source], "z", u * S + d, {"seq": source})

    def ctx_rows(side, c):
        return rows(CROWS * C * side + CROWS * c, CROWS)

    def own_rows(side, c):
        return ctx.at[:, pl.ds(2, NB_SEQ), ctx_rows(side, c), :]

    def forward_copy(c):
        return rc(own_rows(e, c), own_rows(e, c), "fwd", c, partner)

    def prior_copy(c, same_core):
        return rc(
            ctx.at[:, pl.ds(NB_SEQ, 2), ctx_rows(e, c), :],
            ctx.at[:, pl.ds(0, 2), ctx_rows(e, c), :],
            "pr0" if same_core else "pr1", c,
            {"seq": lax.rem(r + 1, S), "enc": e if same_core else pe},
        )

    def encode(u):
        landed(str_.at[u], "st", u, across)
        landed(precv.at[u], "s", u, across)
        c = u // 2
        side = half_of(u)
        other = decoded(precv[u], as_column(str_[u, 0:LINES, :]))
        lined = ss[c, 0:LINES, :] + str_[u, LINES : 2 * LINES, :]
        factor = lax.rsqrt(as_column(lined) / D + epsilon)
        scaled = (sown[c, :, lanes(side)] + other) * factor
        enc[u] = scaled.astype(jnp.bfloat16).reshape(E, CROWS, 128)
        for d in list(range(1, S)) + [0]:
            dst = lax.rem(r + d, S)
            for k in range(cap):
                block = enc[u, pidx[0, dst * cap + k]]
                if d:
                    zs[u, dst, k] = block
                else:
                    zr[c, side, r, k] = block
            if d:
                z_copy(u, d).start()

    def place(c):
        for j in range(2):
            for d in range(1, S):
                z_landed(2 * c + j, d)
        zl[...] = zr[c].reshape(zl.shape)
        for l in list(range(NB_SEQ - 1, -1, -1)):
            where = lidx[0, r * NB_SEQ + l]
            ctx[0, 2 + l, ctx_rows(e, c), :] = zl[0, where]
            ctx[1, 2 + l, ctx_rows(e, c), :] = zl[1, where]

        @pl.when(r < S - 1)
        def _():
            prior_copy(c, True).start()
            prior_copy(c, False).start()

        forward_copy(c).start()

    TL = half // 128
    token_copy = rc(tsend, trecv, "ts", 0, across)
    token_stat = rc(st.at[2 * C], str_.at[2 * C], "st", 2 * C, across)

    def token_pass():
        for i in range(4):
            landed(qpiece(g, i, pe), "wf", i, partner)
            landed(qpiece(pg, i, pe), "wg", i, partner)
        words, peak = coded(product(tb[0], tb[1], woq))
        st[2 * C, 0:TL, :] = as_rows(peak)
        st[2 * C, TL : 2 * TL, :] = ss[C, 0:TL, :]
        token_stat.start()
        tsend[...] = words
        token_copy.start()

    encode(0)
    local_t.wait()
    landed(tb.at[pe], "t", 0, partner)
    local_q.wait()
    landed(wown.at[1, :, lanes(pe)], "wo", 1, partner)
    ss[C, 0:TL, :] = as_rows(squares(tb[0]) + squares(tb[1]))
    town[...] = product(tb[0], tb[1], wown.at[1])
    for i in range(4):
        there = qpiece(pg, i, e)
        landed(there, "wy", i, beside)
        begin(rc(there, there, "wg", i, partner))
    encode(1)

    def middle(c, carry):
        @pl.when(c < C - 1)
        def _():
            other_pass(2 * c + 2)
            other_pass(2 * c + 3)

        @pl.when(c == C - 1)
        def _():
            token_pass()

        encode(2 * c)
        place(c - 1)
        encode(2 * c + 1)
        return carry

    lax.fori_loop(1, C, middle, 0)

    landed(str_.at[2 * C], "st", 2 * C, across)
    landed(trecv, "ts", 0, across)
    lined = ss[C, 0:TL, :] + str_[2 * C, TL : 2 * TL, :]
    factor = lax.rsqrt(as_column(lined) / D + epsilon) * 128 ** (-0.5)
    scaled = (town[...] + decoded(trecv[...], as_column(str_[2 * C, 0:TL, :]))) * factor
    rounded = scaled.astype(jnp.bfloat16)
    low = e == 0
    qb[e] = jnp.where(low, rounded[:, :128], rounded[:, 128:])
    qs[...] = jnp.where(low, rounded[:, 128:], rounded[:, :128])
    begin(rc(qs, qb.at[e], "q", 0, partner))

    place(C - 1)
    landed(qb.at[pe], "q", 0, partner)

    def settle(c, carry):
        landed(own_rows(pe, c), "fwd", c, partner)
        return carry

    lax.fori_loop(0, C, settle, 0)

    spans = half // SPAN

    def attend(c):
        queries = qb[c // spans, rows(c % spans * SPAN, SPAN), :]
        keys = ctx[0, pl.ds(2 * c, 2)].reshape(NBR * RLEN, 128)
        values = ctx[1, pl.ds(2 * c, 2)].reshape(NBR * RLEN, 128)
        scores = lax.dot_general(
            queries, keys, (((1,), (1,)), ((), ())), preferred_element_type=f32
        )
        raised = jnp.exp(scores - jnp.max(scores, axis=1, keepdims=True))
        weight = (raised / jnp.sum(raised, axis=1, keepdims=True)).astype(jnp.bfloat16)
        mixed = jnp.dot(weight, values, preferred_element_type=f32)
        out[rows(c * SPAN, SPAN), :] = mixed.astype(jnp.bfloat16)

    for c in range(1, 2 * spans):
        attend(c)

    def settle_prior(c, carry):
        @pl.when(r > 0)
        def _():
            back = lax.rem(r + S - 1, S)
            landed(ctx.at[:, pl.ds(0, 2), ctx_rows(e, c), :], "pr0", c, {"seq": back})
            landed(ctx.at[:, pl.ds(0, 2), ctx_rows(pe, c), :], "pr1", c, {"seq": back, "enc": pe})

        return carry

    lax.fori_loop(0, C, settle_prior, 0)
    attend(0)

    def drain(c, carry):
        sent_chunk(c).wait_send()
        forward_copy(c).wait_send()

        @pl.when(r < S - 1)
        def _():
            prior_copy(c, True).wait_send()
            prior_copy(c, False).wait_send()

        return carry

    def drain_units(u, carry):
        partial_copy(u).wait_send()
        stat_copy(u).wait_send()
        for d in range(1, S):
            z_copy(u, d).wait_send()
        return carry

    lax.fori_loop(0, C, drain, 0)
    lax.fori_loop(0, 2 * C, drain_units, 0)
    token_copy.wait_send()
    token_stat.wait_send()
    for i in range(4):
        qx(i).wait_send()
    for i in range(8):
        ke(i).wait_send()

    @pl.when(first)
    def _():
        for i in range(4):
            kx(i).wait_send()
            ky(i).wait_send()
        for i in range(8):
            kz(i).wait_send()

    for copy in done:
        copy.wait_send()


def SEMAPHORES(S):
    C = CHUNKS
    return (
        ("kx", 4), ("ky", 4), ("kz", 8), ("ke", 8), ("wo", 2), ("wx", 4), ("wf", 4), ("wy", 4), ("wg", 4),
        ("x", C), ("t", 1), ("s", 2 * C), ("st", 2 * C + 1), ("ts", 1), ("tab", S), ("z", 2 * C * S),
        ("fwd", C), ("pr0", C), ("pr1", C), ("q", 1),
    )


def local_fused(tokens, nbr_feats, counts, slot_target, w_query, w_keyval):
    S = lax.axis_size("seq")
    cap = max(2, 2 * NB_SEQ // S)
    K = tokens.shape[1]
    half = tokens.shape[0] // 2
    C = CHUNKS
    bf, f32, i32 = jnp.bfloat16, jnp.float32, jnp.int32
    anywhere = pl.BlockSpec(memory_space=pl.ANY)
    vmem = pl.BlockSpec(memory_space=pltpu.VMEM)
    count = sum(size for _, size in SEMAPHORES(S))
    return pl.pallas_call(
        functools.partial(fused, S, cap),
        out_shape=jax.ShapeDtypeStruct((2 * half, 128), bf),
        in_specs=[vmem, vmem] + [anywhere] * 4,
        out_specs=vmem,
        scratch_shapes=[
            pltpu.VMEM((2, C, ENC_CAP, CROWS, K), bf),
            pltpu.VMEM((2, half, K), bf),
            pltpu.VMEM((2, 2 * K, 256), bf),
            pltpu.VMEM((2, 2 * K, 128), bf),
            pltpu.VMEM((2 * K, 256), bf),
            pltpu.VMEM((C, CFLAT, 256), f32),
            pltpu.VMEM((2 * C, CFLAT * 3 // 4, 128), i32),
            pltpu.VMEM((2 * C, CFLAT * 3 // 4, 128), i32),
            pltpu.VMEM((half, 256), f32),
            pltpu.VMEM((half * 3 // 4, 256), i32),
            pltpu.VMEM((half * 3 // 4, 256), i32),
            pltpu.VMEM((C + 1, 8, 128), f32),
            pltpu.VMEM((2 * C + 1, 8, 128), f32),
            pltpu.VMEM((2 * C + 1, 8, 128), f32),
            pltpu.VMEM((2 * C, ENC_CAP, CROWS, 128), bf),
            pltpu.VMEM((2 * C, S, cap, CROWS, 128), bf),
            pltpu.VMEM((C, 2, S, cap, CROWS, 128), bf),
            pltpu.VMEM((2, S * cap, CROWS, 128), bf),
            pltpu.VMEM((2, NB_SEQ + 2, RLEN, 128), bf),
            pltpu.VMEM((2, half, 128), bf),
            pltpu.VMEM((half, 128), bf),
            pltpu.VMEM((8, 128), i32),
            pltpu.VMEM((S, 8, 128), i32),
            pltpu.VMEM((8, 128), i32),
            pltpu.VMEM((8, 128), i32),
            pltpu.SMEM((8, 128), i32),
            pltpu.SMEM((8, 128), i32),
            pltpu.SemaphoreType.DMA((C + 5,)),
            pltpu.SemaphoreType.DMA((count,)),
            pltpu.SemaphoreType.DMA((count,)),
        ],
        compiler_params=pltpu.CompilerParams(
            collective_id=0, has_side_effects=True, vmem_limit_bytes=56 << 20
        ),
    )(slot_target.reshape(1, -1), counts.reshape(1, -1), nbr_feats, tokens, w_query, w_keyval)


def solution(mesh):
    small = mesh.shape["mp"] == 2 and mesh.shape["groups"] == 2 and mesh.shape["seq"] == 4
    placed = (
        P(("groups", "seq"), ("mp", "enc")),
        P(("groups", "seq"), None, ("mp", "enc")),
        P("groups"),
        P(("groups", "seq")),
        P(None, ("mp", "enc")),
        P(None, ("mp", "enc")),
    )
    return jax.shard_map(
        local_fused if small else local,
        mesh=mesh,
        in_specs=placed,
        out_specs=P(("groups", "seq"), ("mp", "enc")),
        check_vma=False,
    )
```

```python
import functools
import jax
import jax.numpy as jnp
from jax import lax
from jax.experimental import pallas as pl
from jax.experimental.pallas import tpu as pltpu
from jax.sharding import PartitionSpec as P

D = 4096
SPAN = 64
NBR = 2
RLEN = 128
CH_SEQ = 8
NB_SEQ = 16
ENC_CAP = 24


epsilon = 1e-05


def partner_2(block, axis, stride):
    count = lax.axis_size(axis)
    route = []
    for low in range(count):
        high = low | 1 << stride
        if high != low and high < count:
            route += [(low, high), (high, low)]
    return lax.ppermute(block, axis, route)


def passed_along(block, axis, distance):
    devices = range(lax.axis_size(axis))
    route = [(i - distance, i) for i in devices if i - distance in devices]
    return lax.ppermute(block, axis, route)


def project_fold(weight, piece):
    width = piece.shape[-1]
    flat_rows = piece.reshape(-1, width)
    mine = lax.all_to_all(weight, ("mp", "enc"), split_axis=0, concat_axis=1, tiled=True)
    partial = jnp.dot(flat_rows, mine, preferred_element_type=jnp.float32)
    running = lax.psum_scatter(partial, ("mp", "enc"), scatter_dimension=1, tiled=True)
    widened = flat_rows.astype(jnp.float32)
    squares = lax.psum(jnp.sum(widened * widened, axis=1), ("mp", "enc"))
    return (running, squares)


def normalized(carry, factor):
    running, squares = carry
    scale_rows = lax.rsqrt(squares / D + epsilon) * factor
    return (running * scale_rows[:, None]).astype(jnp.bfloat16)


def routing_plan(slot_target, counts, pair_cap):
    seq_count = counts.shape[0]
    seq_here = lax.axis_index("seq")
    live_count = jnp.sum(jnp.where(jnp.arange(seq_count) == seq_here, counts, 0))
    slot_ids = jnp.arange(ENC_CAP)
    live_slots = slot_ids < live_count
    owner_of = slot_target // NB_SEQ
    position = slot_target % NB_SEQ
    same_owner = (
        (owner_of[:, None] == owner_of[None, :])
        & live_slots[None, :]
        & (slot_ids[None, :] < slot_ids[:, None])
    )
    rank_within = jnp.sum(same_owner.astype(jnp.int32), axis=1)
    target_slot = owner_of * pair_cap + rank_within
    buffer_ids = jnp.arange(seq_count * pair_cap)
    chosen = (buffer_ids[:, None] == target_slot[None, :]) & live_slots[None, :]
    sent_ids = jnp.sum(jnp.where(chosen, position[None, :] + 1, 0), axis=1) - 1
    return (chosen, sent_ids.reshape(seq_count, pair_cap))


def pack_rows(chosen, payload, seq_count, pair_cap):
    packed = jnp.dot(chosen.astype(jnp.bfloat16), payload, preferred_element_type=jnp.float32)
    return packed.astype(jnp.bfloat16).reshape(seq_count, pair_cap, payload.shape[1])


def place_rows(received, received_ids):
    flat_rows = received.reshape(-1, received.shape[-1])
    picker = received_ids.reshape(1, -1) == jnp.arange(NB_SEQ)[:, None]
    placed = jnp.dot(picker.astype(jnp.bfloat16), flat_rows, preferred_element_type=jnp.float32)
    return placed.astype(jnp.bfloat16)


def local(tokens, nbr_feats, counts, slot_target, w_query, w_keyval):
    seq_count = lax.axis_size("seq")
    pair_cap = max(2, 2 * NB_SEQ // seq_count)
    head_size = w_keyval.shape[1]
    chosen, sent_ids = routing_plan(slot_target, counts, pair_cap)
    folded = project_fold(w_keyval, nbr_feats)
    encoded = normalized(folded, 1.0).reshape(ENC_CAP, RLEN * head_size)
    packed = pack_rows(chosen, encoded, seq_count, pair_cap)
    received, received_ids = (
        lax.all_to_all(packed, "seq", split_axis=0, concat_axis=0, tiled=True),
        lax.all_to_all(sent_ids, "seq", split_axis=0, concat_axis=0, tiled=True),
    )
    own_half = place_rows(received, received_ids).reshape(NB_SEQ, RLEN, head_size)
    partner = partner_2(own_half, "enc", 0)
    first_lane = lax.axis_index("enc") == 0
    key_rows = jnp.where(first_lane, own_half, partner).reshape(CH_SEQ, NBR * RLEN, head_size)
    value_rows = jnp.where(first_lane, partner, own_half).reshape(CH_SEQ, NBR * RLEN, head_size)
    prior_keys, prior_values = passed_along((key_rows[-1], value_rows[-1]), "seq", 1)
    context_keys = jnp.concatenate([prior_keys[None], key_rows[:-1]], axis=0)
    context_values = jnp.concatenate([prior_values[None], value_rows[:-1]], axis=0)
    folded_tokens = project_fold(w_query, tokens)
    queries = normalized(folded_tokens, head_size ** (-0.5)).reshape(CH_SEQ, SPAN, head_size)
    scores = jnp.einsum("cqd,ckd->cqk", queries, context_keys, preferred_element_type=jnp.float32)
    weights = jax.nn.softmax(scores, axis=-1).astype(jnp.bfloat16)
    attended = jnp.einsum(
        "cqk,ckd->cqd", weights, context_values, preferred_element_type=jnp.float32
    )
    return attended.astype(jnp.bfloat16).reshape(CH_SEQ * SPAN, head_size)


CHUNKS = 4
CROWS = RLEN // 2 // CHUNKS
CFLAT = ENC_CAP * CROWS
LINES = CFLAT // 128
TOP = 8388600.0


def fused(
    S, cap, trow, cnt, feats, tokens, wq, wkv, out,
    xb, tb, wown, wo, woq, sown, psend, precv, town, tsend, trecv, ss, st, str_,
    enc, zs, zr, zl, ctx, qb, qs, tab, tabr, pidx_v, lidx_v, pidx, lidx,
    lsem, send, recv, ready,
):
    f32, i32 = jnp.float32, jnp.int32
    g, r, m, e = (lax.axis_index(a) for a in ("groups", "seq", "mp", "enc"))
    pg, pm, pe = 1 - g, 1 - m, 1 - e
    p = lax.rem(r, 2)
    first = e == p
    K = feats.shape[2]
    half = tokens.shape[0] // 2
    C = CHUNKS
    Q = K // 4
    partner, across, beside = {"enc": pe}, {"mp": pm}, {"groups": pg}
    paired = {"seq": r + 1 - 2 * p}

    ids = {}
    total = 0
    for name, count in SEMAPHORES(S):
        ids[name] = total
        total += count

    def rc(src, dst, name, at, device):
        i = ids[name] + at
        return pltpu.make_async_remote_copy(
            src_ref=src, dst_ref=dst, send_sem=send.at[i], recv_sem=recv.at[i],
            device_id=device, device_id_type=pl.DeviceIdType.MESH,
        )

    def landed(dst, name, at, device):
        rc(dst, dst, name, at, device).wait_recv()

    def lanes(index):
        return pl.ds(pl.multiple_of(index * 128, 128), 128)

    def rows(start, size):
        return pl.ds(pl.multiple_of(start, 16), size)

    def zpeer(d):
        return (r, r + 1 - 2 * p, lax.rem(r + 2, 4), 3 - r)[d]

    def zdev(d):
        return {"seq": zpeer(d)}

    done = []

    def begin(copy):
        copy.start()
        done.append(copy)

    barrier = pltpu.get_barrier_semaphore()
    above, below = {"seq": lax.rem(r + 1, S)}, {"seq": lax.rem(r + S - 1, S)}

    def signal(semaphore, device):
        pl.semaphore_signal(semaphore, inc=1, device_id=device, device_id_type=pl.DeviceIdType.MESH)

    for device in (across, beside, partner):
        signal(barrier, device)
    pl.when(r < S - 1)(lambda: signal(barrier, above))
    pl.when(r > 0)(lambda: signal(barrier, below))

    def krow(i):
        return rows((K * g if i < 4 else K * pg) + i % 4 * Q, Q)

    def kx(i):
        source = wkv.at[rows(2 * K * pm + K * g + i * Q, Q), :]
        return rc(source, wo.at[e, krow(i)], "kx", i, across)

    def kstep(name, i, device):
        return rc(wo.at[e, krow(i)], wo.at[e, krow(i)], name, i, device)

    def ky(i):
        return kstep("ky", i, beside)

    def kz(i):
        return kstep("kz", i, paired)

    def ke(i):
        return kstep("ke", i, partner)

    def from_across(i):
        landed(wo.at[e, krow(i)], "kx", i, across)
        ky(i).start()
        ke(i).start()
        kz(i).start()

    def from_beside(i):
        landed(wo.at[e, krow(4 + i)], "ky", i, beside)
        ke(4 + i).start()
        kz(4 + i).start()

    def from_paired(i):
        landed(wo.at[e, krow(i)], "kz", i, paired)
        ke(i).start()

    def from_partner():
        for i in range(8):
            landed(wo.at[pe, krow(i)], "ke", i, partner)

    def qpiece(part, i, side):
        return woq.at[rows(part * K + i * Q, Q), lanes(side)]

    def qx(i):
        source = wq.at[rows(2 * K * pm + K * g + i * Q, Q), :]
        return rc(source, qpiece(g, i, e), "wx", i, across)

    weights = (wkv, wq)

    def weight_local(k):
        source = weights[k].at[rows(2 * K * m, 2 * K), :]
        return pltpu.make_async_copy(source, wown.at[k, :, lanes(e)], lsem.at[C + k])

    def weight_sent(k):
        source = weights[k].at[rows(2 * K * m, 2 * K), :]
        return rc(source, wown.at[k, :, lanes(e)], "wo", k, partner)

    def own_chunk(c):
        return pltpu.make_async_copy(
            feats.at[:, rows(CROWS * C * e + CROWS * c, CROWS), :], xb.at[e, c], lsem.at[c]
        )

    def sent_chunk(c):
        return rc(
            feats.at[:, rows(CROWS * C * pe + CROWS * c, CROWS), :], xb.at[e, c], "x", c, partner
        )

    local_kv = weight_local(0)
    local_kv.start()
    for c in range(C):
        own_chunk(c).start()
    local_q = weight_local(1)
    local_q.start()
    local_t = pltpu.make_async_copy(tokens.at[rows(half * e, half), :], tb.at[e], lsem.at[C + 2])
    local_t.start()

    pl.semaphore_wait(barrier, 3 + jnp.where(r > 0, 1, 0) + jnp.where(r < S - 1, 1, 0))

    @pl.when(jnp.logical_and(r > 0, r < S - 1))
    def _():
        signal(ready.at[0], above)
        signal(ready.at[1], below)

    @pl.when(first)
    def _():
        for i in range(4):
            kx(i).start()
        for i in range(4):
            qx(i).start()

    begin(weight_sent(0))
    sent_chunk(0).start()
    sent_chunk(1).start()

    t_row = trow[...]
    iota = lambda shape, axis: lax.broadcasted_iota(jnp.int32, shape, axis)
    E = ENC_CAP
    t_col = jnp.sum(jnp.where(iota((E, E), 0) == iota((E, E), 1), t_row, 0), axis=1, keepdims=True)
    live = jnp.sum(jnp.where(iota((1, S), 1) == r, cnt[...], 0), axis=1, keepdims=True)
    same = (
        ((t_col >> 4) == (t_row >> 4)) & (iota((E, E), 1) < live) & (iota((E, E), 1) < iota((E, E), 0))
    )
    rank = jnp.sum(jnp.where(same, 1, 0), axis=1, keepdims=True)
    at_lane = iota((E, 128), 1)
    slot = iota((E, 128), 0)
    is_live = slot < live
    wanted = ((t_col >> 4) * cap + rank == at_lane) & is_live
    source_row = jnp.sum(jnp.where(wanted, slot, 0), axis=0, keepdims=True)
    held = (t_col == at_lane) & is_live
    place_row = jnp.sum(jnp.where(held, r * cap + rank, 0), axis=0, keepdims=True)
    pidx_v[...] = jnp.broadcast_to(source_row, (8, 128))
    tab[...] = jnp.broadcast_to(place_row, (8, 128))
    pack_copy = pltpu.make_async_copy(pidx_v, pidx, lsem.at[C + 3])
    pack_copy.start()
    tabr[0] = tab[...]
    ss[...] = jnp.zeros_like(ss)
    st[...] = jnp.zeros_like(st)

    @pl.when(r == 0)
    def _():
        ctx[:, 0:2] = jnp.zeros((2, 2) + ctx.shape[2:], ctx.dtype)

    @pl.when(r > 1)
    def _():
        pl.semaphore_wait(ready.at[0], 1)
        pl.when(r < S - 1)(lambda: signal(ready.at[2], above))
        pl.when(r == S - 1)(lambda: pl.semaphore_wait(ready.at[2], 1))

    @pl.when(r < S - 2)
    def _():
        pl.semaphore_wait(ready.at[1], 1)
        pl.when(r > 0)(lambda: signal(ready.at[3], below))
        pl.when(r == 0)(lambda: pl.semaphore_wait(ready.at[3], 1))

    for d in range(1, S):
        begin(rc(tab, tabr.at[d], "tab", d, zdev(d)))

    eye = iota((128, 128), 0) == iota((128, 128), 1)

    def as_rows(column):
        blocks = column.reshape(-1, 128, 1)
        return jnp.sum(jnp.where(eye[None], blocks, 0.0), axis=1)

    def as_column(lined):
        blocks = jnp.where(eye[None], lined[:, None, :], 0.0)
        return jnp.sum(blocks, axis=2, keepdims=True).reshape(-1, 1)

    def squares(block):
        wide = block.astype(f32)
        return jnp.sum(wide * wide, axis=1, keepdims=True)

    def product(one, two, weight):
        return jnp.dot(one, weight[:K, :], preferred_element_type=f32) + jnp.dot(
            two, weight[K:, :], preferred_element_type=f32
        )

    def chunk_rows(c):
        return xb[0, c].reshape(CFLAT, K), xb[1, c].reshape(CFLAT, K)

    def own_pass(c):
        own_chunk(c).wait()
        landed(xb.at[pe, c], "x", c, partner)
        one, two = chunk_rows(c)
        ss[c, 0:LINES, :] = as_rows(squares(one) + squares(two))
        sown[c] = product(one, two, wown.at[0])

    def coded(part):
        peak = jnp.maximum(jnp.max(jnp.abs(part), axis=1, keepdims=True), 1e-30)
        whole = jnp.floor(part * (TOP / peak) + 0.5).astype(i32)
        block = part.shape[0] // 4
        last = whole[3 * block :]
        words = [
            (whole[i * block : (i + 1) * block] << 8) | ((last >> (8 * i)) & 255) for i in range(3)
        ]
        return jnp.concatenate(words, axis=0), peak

    def decoded(words, peak):
        block = words.shape[0] // 3
        parts = [words[i * block : (i + 1) * block] for i in range(3)]
        last = ((parts[2] << 24) >> 8) | ((parts[1] & 255) << 8) | (parts[0] & 255)
        whole = jnp.concatenate([word >> 8 for word in parts] + [last], axis=0)
        return whole.astype(f32) * (peak * (1.0 / TOP))

    def half_of(u):
        return lax.rem(u + p, 2)

    def partial_copy(u):
        return rc(psend.at[u], precv.at[u], "s", u, across)

    def stat_copy(u):
        return rc(st.at[u], str_.at[u], "st", u, across)

    def other_pass(u):
        c = u // 2
        one, two = chunk_rows(c)
        words, peak = coded(product(one, two, wo.at[half_of(u)]))
        st[u, 0:LINES, :] = as_rows(peak)
        st[u, LINES : 2 * LINES, :] = ss[c, 0:LINES, :]
        stat_copy(u).start()
        psend[u] = words
        partial_copy(u).start()

    @pl.when(first)
    def _():
        from_across(0)

    local_kv.wait()
    landed(wown.at[0, :, lanes(pe)], "wo", 0, partner)
    own_pass(0)

    @pl.when(first)
    def _():
        from_across(1)
        from_across(2)

    @pl.when(jnp.logical_not(first))
    def _():
        for i in range(4):
            qx(i).start()

    sent_chunk(2).start()
    own_pass(1)

    @pl.when(first)
    def _():
        from_across(3)
        for i in range(4):
            from_beside(i)

    @pl.when(jnp.logical_not(first))
    def _():
        for i in range(4):
            from_paired(i)
        from_partner()

    other_pass(0)

    @pl.when(jnp.logical_not(first))
    def _():
        for i in range(4, 8):
            from_paired(i)

    sent_chunk(3).start()

    @pl.when(first)
    def _():
        from_partner()

    other_pass(1)
    begin(weight_sent(1))
    begin(rc(tokens.at[rows(half * pe, half), :], tb.at[e], "t", 0, partner))
    own_pass(2)
    own_pass(3)

    def other_two(u, carry):
        other_pass(u)
        return carry

    lax.fori_loop(2, 4, other_two, 0)

    for i in range(4):
        here = qpiece(g, i, e)
        landed(here, "wx", i, across)
        begin(rc(here, here, "wy", i, beside))
        begin(rc(here, here, "wf", i, partner))

    for d in range(1, S):
        landed(tabr.at[d], "tab", d, zdev(d))
    places = tabr[0]
    for d in range(1, S):
        places = places + tabr[d]
    lidx_v[...] = places
    place_copy = pltpu.make_async_copy(lidx_v, lidx, lsem.at[C + 4])
    place_copy.start()
    pack_copy.wait()
    place_copy.wait()

    def z_copy(u, d):
        dst = zpeer(d)
        return rc(zs.at[u, dst], zr.at[u // 2, half_of(u), r], "z", u * S + d, zdev(d))

    def z_landed(u, d):
        source = zpeer(d)
        side = lax.rem(u + lax.rem(source, 2), 2)
        landed(zr.at[u // 2, side, source], "z", u * S + d, {"seq": source})

    def ctx_rows(side, c):
        return rows(CROWS * C * side + CROWS * c, CROWS)

    def own_rows(side, c):
        return ctx.at[:, pl.ds(2, NB_SEQ), ctx_rows(side, c), :]

    def forward_copy(c):
        return rc(own_rows(e, c), own_rows(e, c), "fwd", c, partner)

    def prior_copy(c, same_core):
        return rc(
            ctx.at[:, pl.ds(NB_SEQ, 2), ctx_rows(e, c), :],
            ctx.at[:, pl.ds(0, 2), ctx_rows(e, c), :],
            "pr0" if same_core else "pr1", c,
            {"seq": lax.rem(r + 1, S), "enc": e if same_core else pe},
        )

    def encode(u):
        landed(str_.at[u], "st", u, across)
        landed(precv.at[u], "s", u, across)
        c = u // 2
        side = half_of(u)
        other = decoded(precv[u], as_column(str_[u, 0:LINES, :]))
        lined = ss[c, 0:LINES, :] + str_[u, LINES : 2 * LINES, :]
        factor = lax.rsqrt(as_column(lined) / D + epsilon)
        scaled = (sown[c, :, lanes(side)] + other) * factor
        enc[u] = scaled.astype(jnp.bfloat16).reshape(E, CROWS, 128)
        for d in (3, 2, 1, 0):
            dst = zpeer(d)
            for k in range(cap):
                block = enc[u, pidx[0, dst * cap + k]]
                if d:
                    zs[u, dst, k] = block
                else:
                    zr[c, side, r, k] = block
            if d:
                z_copy(u, d).start()

    def place(c):
        for j in range(2):
            for d in range(1, S):
                z_landed(2 * c + j, d)
        zl[...] = zr[c].reshape(zl.shape)

        def put(l):
            where = lidx[0, r * NB_SEQ + l]
            ctx[0, 2 + l, ctx_rows(e, c), :] = zl[0, where]
            ctx[1, 2 + l, ctx_rows(e, c), :] = zl[1, where]

        put(NB_SEQ - 1)
        put(NB_SEQ - 2)

        @pl.when(r < S - 1)
        def _():
            prior_copy(c, True).start()
            prior_copy(c, False).start()

        for l in range(NB_SEQ - 2):
            put(l)

        forward_copy(c).start()

    TL = half // 128
    token_copy = rc(tsend, trecv, "ts", 0, across)
    token_stat = rc(st.at[2 * C], str_.at[2 * C], "st", 2 * C, across)

    def token_pass():
        for i in range(4):
            landed(qpiece(g, i, pe), "wf", i, partner)
            landed(qpiece(pg, i, pe), "wg", i, partner)
        words, peak = coded(product(tb[0], tb[1], woq))
        st[2 * C, 0:TL, :] = as_rows(peak)
        st[2 * C, TL : 2 * TL, :] = ss[C, 0:TL, :]
        token_stat.start()
        tsend[...] = words
        token_copy.start()

    encode(0)
    local_t.wait()
    landed(tb.at[pe], "t", 0, partner)
    local_q.wait()
    landed(wown.at[1, :, lanes(pe)], "wo", 1, partner)
    ss[C, 0:TL, :] = as_rows(squares(tb[0]) + squares(tb[1]))
    town[...] = product(tb[0], tb[1], wown.at[1])
    for i in range(4):
        there = qpiece(pg, i, e)
        landed(there, "wy", i, beside)
        begin(rc(there, there, "wg", i, partner))
    encode(1)

    def middle(c, carry):
        @pl.when(c < C - 1)
        def _():
            other_pass(2 * c + 2)
            other_pass(2 * c + 3)

        @pl.when(c == C - 1)
        def _():
            token_pass()

        encode(2 * c)
        place(c - 1)
        encode(2 * c + 1)
        return carry

    lax.fori_loop(1, C, middle, 0)

    landed(str_.at[2 * C], "st", 2 * C, across)
    landed(trecv, "ts", 0, across)
    lined = ss[C, 0:TL, :] + str_[2 * C, TL : 2 * TL, :]
    factor = lax.rsqrt(as_column(lined) / D + epsilon) * 128 ** (-0.5)
    scaled = (town[...] + decoded(trecv[...], as_column(str_[2 * C, 0:TL, :]))) * factor
    rounded = scaled.astype(jnp.bfloat16)
    low = e == 0
    qb[e] = jnp.where(low, rounded[:, :128], rounded[:, 128:])
    qs[...] = jnp.where(low, rounded[:, 128:], rounded[:, :128])
    begin(rc(qs, qb.at[e], "q", 0, partner))

    place(C - 1)
    landed(qb.at[pe], "q", 0, partner)

    def settle(c, carry):
        landed(own_rows(pe, c), "fwd", c, partner)
        return carry

    lax.fori_loop(0, C, settle, 0)

    spans = half // SPAN

    def attend(those):
        scores = []
        for c in those:
            queries = qb[c // spans, rows(c % spans * SPAN, SPAN), :]
            keys = ctx[0, pl.ds(2 * c, 2)].reshape(NBR * RLEN, 128)
            scores.append(
                lax.dot_general(
                    queries, keys, (((1,), (1,)), ((), ())), preferred_element_type=f32
                )
            )
        raised = [jnp.exp(s - jnp.max(s, axis=1, keepdims=True)) for s in scores]
        weight = [(x / jnp.sum(x, axis=1, keepdims=True)).astype(jnp.bfloat16) for x in raised]
        for c, w in zip(those, weight):
            values = ctx[1, pl.ds(2 * c, 2)].reshape(NBR * RLEN, 128)
            mixed = jnp.dot(w, values, preferred_element_type=f32)
            out[rows(c * SPAN, SPAN), :] = mixed.astype(jnp.bfloat16)

    attend(range(1, 2 * spans))

    def settle_prior(c, carry):
        @pl.when(r > 0)
        def _():
            back = lax.rem(r + S - 1, S)
            landed(ctx.at[:, pl.ds(0, 2), ctx_rows(e, c), :], "pr0", c, {"seq": back})
            landed(ctx.at[:, pl.ds(0, 2), ctx_rows(pe, c), :], "pr1", c, {"seq": back, "enc": pe})

        return carry

    lax.fori_loop(0, C, settle_prior, 0)
    attend([0])

    def drain(c, carry):
        sent_chunk(c).wait_send()
        forward_copy(c).wait_send()

        @pl.when(r < S - 1)
        def _():
            prior_copy(c, True).wait_send()
            prior_copy(c, False).wait_send()

        return carry

    def drain_units(u, carry):
        partial_copy(u).wait_send()
        stat_copy(u).wait_send()
        for d in range(1, S):
            z_copy(u, d).wait_send()
        return carry

    lax.fori_loop(0, C, drain, 0)
    lax.fori_loop(0, 2 * C, drain_units, 0)
    token_copy.wait_send()
    token_stat.wait_send()
    for i in range(4):
        qx(i).wait_send()
    for i in range(8):
        ke(i).wait_send()

    @pl.when(first)
    def _():
        for i in range(4):
            kx(i).wait_send()
            ky(i).wait_send()
        for i in range(8):
            kz(i).wait_send()

    for copy in done:
        copy.wait_send()


def SEMAPHORES(S):
    C = CHUNKS
    return (
        ("kx", 4), ("ky", 4), ("kz", 8), ("ke", 8), ("wo", 2), ("wx", 4), ("wf", 4), ("wy", 4), ("wg", 4),
        ("x", C), ("t", 1), ("s", 2 * C), ("st", 2 * C + 1), ("ts", 1), ("tab", S), ("z", 2 * C * S),
        ("fwd", C), ("pr0", C), ("pr1", C), ("q", 1),
    )


def local_fused(tokens, nbr_feats, counts, slot_target, w_query, w_keyval):
    S = lax.axis_size("seq")
    cap = max(2, 2 * NB_SEQ // S)
    K = tokens.shape[1]
    half = tokens.shape[0] // 2
    C = CHUNKS
    bf, f32, i32 = jnp.bfloat16, jnp.float32, jnp.int32
    anywhere = pl.BlockSpec(memory_space=pl.ANY)
    vmem = pl.BlockSpec(memory_space=pltpu.VMEM)
    count = sum(size for _, size in SEMAPHORES(S))
    return pl.pallas_call(
        functools.partial(fused, S, cap),
        out_shape=jax.ShapeDtypeStruct((2 * half, 128), bf),
        in_specs=[vmem, vmem] + [anywhere] * 4,
        out_specs=vmem,
        scratch_shapes=[
            pltpu.VMEM((2, C, ENC_CAP, CROWS, K), bf),
            pltpu.VMEM((2, half, K), bf),
            pltpu.VMEM((2, 2 * K, 256), bf),
            pltpu.VMEM((2, 2 * K, 128), bf),
            pltpu.VMEM((2 * K, 256), bf),
            pltpu.VMEM((C, CFLAT, 256), f32),
            pltpu.VMEM((2 * C, CFLAT * 3 // 4, 128), i32),
            pltpu.VMEM((2 * C, CFLAT * 3 // 4, 128), i32),
            pltpu.VMEM((half, 256), f32),
            pltpu.VMEM((half * 3 // 4, 256), i32),
            pltpu.VMEM((half * 3 // 4, 256), i32),
            pltpu.VMEM((C + 1, 8, 128), f32),
            pltpu.VMEM((2 * C + 1, 8, 128), f32),
            pltpu.VMEM((2 * C + 1, 8, 128), f32),
            pltpu.VMEM((2 * C, ENC_CAP, CROWS, 128), bf),
            pltpu.VMEM((2 * C, S, cap, CROWS, 128), bf),
            pltpu.VMEM((C, 2, S, cap, CROWS, 128), bf),
            pltpu.VMEM((2, S * cap, CROWS, 128), bf),
            pltpu.VMEM((2, NB_SEQ + 2, RLEN, 128), bf),
            pltpu.VMEM((2, half, 128), bf),
            pltpu.VMEM((half, 128), bf),
            pltpu.VMEM((8, 128), i32),
            pltpu.VMEM((S, 8, 128), i32),
            pltpu.VMEM((8, 128), i32),
            pltpu.VMEM((8, 128), i32),
            pltpu.SMEM((8, 128), i32),
            pltpu.SMEM((8, 128), i32),
            pltpu.SemaphoreType.DMA((C + 5,)),
            pltpu.SemaphoreType.DMA((count,)),
            pltpu.SemaphoreType.DMA((count,)),
            pltpu.SemaphoreType.REGULAR((4,)),
        ],
        compiler_params=pltpu.CompilerParams(
            collective_id=0, has_side_effects=True, vmem_limit_bytes=56 << 20
        ),
    )(slot_target.reshape(1, -1), counts.reshape(1, -1), nbr_feats, tokens, w_query, w_keyval)


def solution(mesh):
    small = mesh.shape["mp"] == 2 and mesh.shape["groups"] == 2 and mesh.shape["seq"] == 4
    placed = (
        P(("groups", "seq"), ("mp", "enc")),
        P(("groups", "seq"), None, ("mp", "enc")),
        P("groups"),
        P(("groups", "seq")),
        P(None, ("mp", "enc")),
        P(None, ("mp", "enc")),
    )
    return jax.shard_map(
        local_fused if small else local,
        mesh=mesh,
        in_specs=placed,
        out_specs=P(("groups", "seq"), ("mp", "enc")),
        check_vma=False,
    )
```

```python
import functools
import jax
import jax.numpy as jnp
from jax import lax
from jax.experimental import pallas as pl
from jax.experimental.pallas import tpu as pltpu
from jax.sharding import PartitionSpec as P

D = 4096
SPAN = 64
NBR = 2
RLEN = 128
CH_SEQ = 8
NB_SEQ = 16
ENC_CAP = 24


epsilon = 1e-05


def partner_2(block, axis, stride):
    count = lax.axis_size(axis)
    route = []
    for low in range(count):
        high = low | 1 << stride
        if high != low and high < count:
            route += [(low, high), (high, low)]
    return lax.ppermute(block, axis, route)


def passed_along(block, axis, distance):
    devices = range(lax.axis_size(axis))
    route = [(i - distance, i) for i in devices if i - distance in devices]
    return lax.ppermute(block, axis, route)


def project_fold(weight, piece):
    width = piece.shape[-1]
    flat_rows = piece.reshape(-1, width)
    mine = lax.all_to_all(weight, ("mp", "enc"), split_axis=0, concat_axis=1, tiled=True)
    partial = jnp.dot(flat_rows, mine, preferred_element_type=jnp.float32)
    running = lax.psum_scatter(partial, ("mp", "enc"), scatter_dimension=1, tiled=True)
    widened = flat_rows.astype(jnp.float32)
    squares = lax.psum(jnp.sum(widened * widened, axis=1), ("mp", "enc"))
    return (running, squares)


def normalized(carry, factor):
    running, squares = carry
    scale_rows = lax.rsqrt(squares / D + epsilon) * factor
    return (running * scale_rows[:, None]).astype(jnp.bfloat16)


def routing_plan(slot_target, counts, pair_cap):
    seq_count = counts.shape[0]
    seq_here = lax.axis_index("seq")
    live_count = jnp.sum(jnp.where(jnp.arange(seq_count) == seq_here, counts, 0))
    slot_ids = jnp.arange(ENC_CAP)
    live_slots = slot_ids < live_count
    owner_of = slot_target // NB_SEQ
    position = slot_target % NB_SEQ
    same_owner = (
        (owner_of[:, None] == owner_of[None, :])
        & live_slots[None, :]
        & (slot_ids[None, :] < slot_ids[:, None])
    )
    rank_within = jnp.sum(same_owner.astype(jnp.int32), axis=1)
    target_slot = owner_of * pair_cap + rank_within
    buffer_ids = jnp.arange(seq_count * pair_cap)
    chosen = (buffer_ids[:, None] == target_slot[None, :]) & live_slots[None, :]
    sent_ids = jnp.sum(jnp.where(chosen, position[None, :] + 1, 0), axis=1) - 1
    return (chosen, sent_ids.reshape(seq_count, pair_cap))


def pack_rows(chosen, payload, seq_count, pair_cap):
    packed = jnp.dot(chosen.astype(jnp.bfloat16), payload, preferred_element_type=jnp.float32)
    return packed.astype(jnp.bfloat16).reshape(seq_count, pair_cap, payload.shape[1])


def place_rows(received, received_ids):
    flat_rows = received.reshape(-1, received.shape[-1])
    picker = received_ids.reshape(1, -1) == jnp.arange(NB_SEQ)[:, None]
    placed = jnp.dot(picker.astype(jnp.bfloat16), flat_rows, preferred_element_type=jnp.float32)
    return placed.astype(jnp.bfloat16)


def local(tokens, nbr_feats, counts, slot_target, w_query, w_keyval):
    seq_count = lax.axis_size("seq")
    pair_cap = max(2, 2 * NB_SEQ // seq_count)
    head_size = w_keyval.shape[1]
    chosen, sent_ids = routing_plan(slot_target, counts, pair_cap)
    folded = project_fold(w_keyval, nbr_feats)
    encoded = normalized(folded, 1.0).reshape(ENC_CAP, RLEN * head_size)
    packed = pack_rows(chosen, encoded, seq_count, pair_cap)
    received, received_ids = (
        lax.all_to_all(packed, "seq", split_axis=0, concat_axis=0, tiled=True),
        lax.all_to_all(sent_ids, "seq", split_axis=0, concat_axis=0, tiled=True),
    )
    own_half = place_rows(received, received_ids).reshape(NB_SEQ, RLEN, head_size)
    partner = partner_2(own_half, "enc", 0)
    first_lane = lax.axis_index("enc") == 0
    key_rows = jnp.where(first_lane, own_half, partner).reshape(CH_SEQ, NBR * RLEN, head_size)
    value_rows = jnp.where(first_lane, partner, own_half).reshape(CH_SEQ, NBR * RLEN, head_size)
    prior_keys, prior_values = passed_along((key_rows[-1], value_rows[-1]), "seq", 1)
    context_keys = jnp.concatenate([prior_keys[None], key_rows[:-1]], axis=0)
    context_values = jnp.concatenate([prior_values[None], value_rows[:-1]], axis=0)
    folded_tokens = project_fold(w_query, tokens)
    queries = normalized(folded_tokens, head_size ** (-0.5)).reshape(CH_SEQ, SPAN, head_size)
    scores = jnp.einsum("cqd,ckd->cqk", queries, context_keys, preferred_element_type=jnp.float32)
    weights = jax.nn.softmax(scores, axis=-1).astype(jnp.bfloat16)
    attended = jnp.einsum(
        "cqk,ckd->cqd", weights, context_values, preferred_element_type=jnp.float32
    )
    return attended.astype(jnp.bfloat16).reshape(CH_SEQ * SPAN, head_size)


CHUNKS = 4
CROWS = RLEN // 2 // CHUNKS
CFLAT = ENC_CAP * CROWS
LINES = CFLAT // 128
TOP = 8388600.0


def fused(
    S, cap, trow, cnt, feats, tokens, wq, wkv, out,
    xb, tb, wown, wo, woq, sown, psend, precv, town, tsend, trecv, ss, st, str_,
    enc, zs, zr, zl, ctx, qb, qs, tab, tabr, pidx_v, lidx_v, pidx, lidx,
    lsem, send, recv, ready,
):
    f32, i32 = jnp.float32, jnp.int32
    g, r, m, e = (lax.axis_index(a) for a in ("groups", "seq", "mp", "enc"))
    pg, pm, pe = 1 - g, 1 - m, 1 - e
    p = lax.rem(r, 2)
    first = e == p
    K = feats.shape[2]
    half = tokens.shape[0] // 2
    C = CHUNKS
    Q = K // 4
    partner, across, beside = {"enc": pe}, {"mp": pm}, {"groups": pg}
    paired = {"seq": r + 1 - 2 * p}

    ids = {}
    total = 0
    for name, count in SEMAPHORES(S):
        ids[name] = total
        total += count

    def rc(src, dst, name, at, device):
        i = ids[name] + at
        return pltpu.make_async_remote_copy(
            src_ref=src, dst_ref=dst, send_sem=send.at[i], recv_sem=recv.at[i],
            device_id=device, device_id_type=pl.DeviceIdType.MESH,
        )

    def landed(dst, name, at, device):
        rc(dst, dst, name, at, device).wait_recv()

    def lanes(index):
        return pl.ds(pl.multiple_of(index * 128, 128), 128)

    def rows(start, size):
        return pl.ds(pl.multiple_of(start, 16), size)

    def zpeer(d):
        return (r, r + 1 - 2 * p, lax.rem(r + 2, 4), 3 - r)[d]

    def zdev(d):
        return {"seq": zpeer(d)}

    done = []

    def begin(copy):
        copy.start()
        done.append(copy)

    barrier = pltpu.get_barrier_semaphore()
    above, below = {"seq": lax.rem(r + 1, S)}, {"seq": lax.rem(r + S - 1, S)}

    def signal(semaphore, device):
        pl.semaphore_signal(semaphore, inc=1, device_id=device, device_id_type=pl.DeviceIdType.MESH)

    for device in (across, beside, partner):
        signal(barrier, device)
    pl.when(r < S - 1)(lambda: signal(barrier, above))
    pl.when(r > 0)(lambda: signal(barrier, below))

    def kstart(i):
        return (K * g if i < 4 else K * pg) + i % 4 * Q

    def krow(i):
        return rows(kstart(i), Q)

    def kx(i):
        source = wkv.at[rows(2 * K * pm + kstart(i), Q), :]
        return rc(source, wo.at[e, krow(i)], "kx", i, across)

    def ky(i):
        return rc(wo.at[e, krow(i)], wo.at[e, krow(i)], "ky", i, beside)

    def kz(i):
        return rc(wo.at[e, krow(i)], wo.at[e, krow(i)], "kz", i, paired)

    def ke(i):
        return rc(wo.at[e, krow(i)], wo.at[e, krow(i)], "ke", i, partner)

    def from_across(i):
        landed(wo.at[e, krow(i)], "kx", i, across)
        if i < 3:
            ky(i).start()
        ke(i).start()
        kz(i).start()

    def from_beside(i):
        landed(wo.at[e, krow(4 + i)], "ky", i, beside)
        ke(4 + i).start()
        kz(4 + i).start()

    def from_paired(i):
        landed(wo.at[e, krow(i)], "kz", i, paired)
        ke(i).start()

    def from_partner():
        for i in range(8):
            landed(wo.at[pe, krow(i)], "ke", i, partner)

    def qpiece(i, side):
        start = (K * g if i < 4 else K * pg) + i % 4 * Q
        return woq.at[rows(start, Q), lanes(side)]

    def qx(i):
        source = wq.at[rows(2 * K * pm + K * g + i * Q, Q), :]
        return rc(source, qpiece(i, e), "qx", i, across)

    def qstep(name, i, device):
        return rc(qpiece(i, e), qpiece(i, e), name, i, device)

    def q_across(i):
        landed(qpiece(i, e), "qx", i, across)
        qstep("qy", i, beside).start()
        qstep("qe", i, partner).start()
        qstep("qz", i, paired).start()

    def q_beside(i):
        landed(qpiece(4 + i, e), "qy", i, beside)
        qstep("qe", 4 + i, partner).start()
        qstep("qz", 4 + i, paired).start()

    def q_paired(i):
        landed(qpiece(i, e), "qz", i, paired)
        qstep("qe", i, partner).start()

    weights = (wkv, wq)

    def weight_local(k):
        source = weights[k].at[rows(2 * K * m, 2 * K), :]
        return pltpu.make_async_copy(source, wown.at[k, :, lanes(e)], lsem.at[C + k])

    def weight_sent(k):
        source = weights[k].at[rows(2 * K * m, 2 * K), :]
        return rc(source, wown.at[k, :, lanes(e)], "wo", k, partner)

    def own_chunk(c):
        return pltpu.make_async_copy(
            feats.at[:, rows(CROWS * C * e + CROWS * c, CROWS), :], xb.at[e, c], lsem.at[c]
        )

    def sent_chunk(c):
        return rc(
            feats.at[:, rows(CROWS * C * pe + CROWS * c, CROWS), :], xb.at[e, c], "x", c, partner
        )

    local_kv = weight_local(0)
    local_kv.start()
    for c in range(C):
        own_chunk(c).start()
    local_q = weight_local(1)
    local_q.start()
    local_t = pltpu.make_async_copy(tokens.at[rows(half * e, half), :], tb.at[e], lsem.at[C + 2])
    local_t.start()

    pl.semaphore_wait(barrier, 3 + jnp.where(r > 0, 1, 0) + jnp.where(r < S - 1, 1, 0))

    @pl.when(jnp.logical_and(r > 0, r < S - 1))
    def _():
        signal(ready.at[0], above)
        signal(ready.at[1], below)

    @pl.when(first)
    def _():
        for i in (0, 1, 2, 3, 7):
            kx(i).start()
        for i in range(4):
            qx(i).start()

    begin(weight_sent(0))
    sent_chunk(0).start()
    sent_chunk(1).start()

    t_row = trow[...]
    iota = lambda shape, axis: lax.broadcasted_iota(jnp.int32, shape, axis)
    E = ENC_CAP
    t_col = jnp.sum(jnp.where(iota((E, E), 0) == iota((E, E), 1), t_row, 0), axis=1, keepdims=True)
    live = jnp.sum(jnp.where(iota((1, S), 1) == r, cnt[...], 0), axis=1, keepdims=True)
    same = (
        ((t_col >> 4) == (t_row >> 4)) & (iota((E, E), 1) < live) & (iota((E, E), 1) < iota((E, E), 0))
    )
    rank = jnp.sum(jnp.where(same, 1, 0), axis=1, keepdims=True)
    at_lane = iota((E, 128), 1)
    slot = iota((E, 128), 0)
    is_live = slot < live
    wanted = ((t_col >> 4) * cap + rank == at_lane) & is_live
    source_row = jnp.sum(jnp.where(wanted, slot, 0), axis=0, keepdims=True)
    held = (t_col == at_lane) & is_live
    place_row = jnp.sum(jnp.where(held, r * cap + rank, 0), axis=0, keepdims=True)
    pidx_v[...] = jnp.broadcast_to(source_row, (8, 128))
    tab[...] = jnp.broadcast_to(place_row, (8, 128))
    pack_copy = pltpu.make_async_copy(pidx_v, pidx, lsem.at[C + 3])
    pack_copy.start()
    tabr[0] = tab[...]
    ss[...] = jnp.zeros_like(ss)
    st[...] = jnp.zeros_like(st)

    @pl.when(r == 0)
    def _():
        ctx[:, 0:2] = jnp.zeros((2, 2) + ctx.shape[2:], ctx.dtype)

    eye = iota((128, 128), 0) == iota((128, 128), 1)

    def as_rows(column):
        blocks = column.reshape(-1, 128, 1)
        return jnp.sum(jnp.where(eye[None], blocks, 0.0), axis=1)

    def as_column(lined):
        blocks = jnp.where(eye[None], lined[:, None, :], 0.0)
        return jnp.sum(blocks, axis=2, keepdims=True).reshape(-1, 1)

    def squares(block):
        wide = block.astype(f32)
        return jnp.sum(wide * wide, axis=1, keepdims=True)

    def product(one, two, weight):
        return jnp.dot(one, weight[:K, :], preferred_element_type=f32) + jnp.dot(
            two, weight[K:, :], preferred_element_type=f32
        )

    def chunk_rows(c):
        return xb[0, c].reshape(CFLAT, K), xb[1, c].reshape(CFLAT, K)

    def own_pass(c):
        own_chunk(c).wait()
        landed(xb.at[pe, c], "x", c, partner)
        one, two = chunk_rows(c)
        ss[c, 0:LINES, :] = as_rows(squares(one) + squares(two))
        sown[c] = product(one, two, wown.at[0])

    def coded(part):
        peak = jnp.maximum(jnp.max(jnp.abs(part), axis=1, keepdims=True), 1e-30)
        whole = jnp.floor(part * (TOP / peak) + 0.5).astype(i32)
        block = part.shape[0] // 4
        last = whole[3 * block :]
        words = [
            (whole[i * block : (i + 1) * block] << 8) | ((last >> (8 * i)) & 255) for i in range(3)
        ]
        return jnp.concatenate(words, axis=0), peak

    def decoded(words, peak):
        block = words.shape[0] // 3
        parts = [words[i * block : (i + 1) * block] for i in range(3)]
        last = ((parts[2] << 24) >> 8) | ((parts[1] & 255) << 8) | (parts[0] & 255)
        whole = jnp.concatenate([word >> 8 for word in parts] + [last], axis=0)
        return whole.astype(f32) * (peak * (1.0 / TOP))

    def half_of(u):
        return lax.rem(u + p, 2)

    def partial_copy(u):
        return rc(psend.at[u], precv.at[u], "s", u, across)

    def stat_copy(u):
        return rc(st.at[u], str_.at[u], "st", u, across)

    def other_pass(u):
        c = u // 2
        one, two = chunk_rows(c)
        words, peak = coded(product(one, two, wo.at[half_of(u)]))
        st[u, 0:LINES, :] = as_rows(peak)
        st[u, LINES : 2 * LINES, :] = ss[c, 0:LINES, :]
        stat_copy(u).start()
        psend[u] = words
        partial_copy(u).start()

    @pl.when(first)
    def _():
        from_across(0)

    local_kv.wait()
    landed(wown.at[0, :, lanes(pe)], "wo", 0, partner)
    own_pass(0)

    @pl.when(r > 1)
    def _():
        pl.semaphore_wait(ready.at[0], 1)
        pl.when(r < S - 1)(lambda: signal(ready.at[2], above))

    @pl.when(r < S - 2)
    def _():
        pl.semaphore_wait(ready.at[1], 1)
        pl.when(r > 0)(lambda: signal(ready.at[3], below))

    @pl.when(first)
    def _():
        for i in range(1, 4):
            from_across(i)

    sent_chunk(2).start()
    own_pass(1)

    @pl.when(first)
    def _():
        from_across(7)
        for i in range(3):
            from_beside(i)

    @pl.when(jnp.logical_not(first))
    def _():
        for i in range(3):
            from_paired(i)
        from_partner()

    other_pass(0)
    sent_chunk(3).start()

    @pl.when(first)
    def _():
        for i in range(4):
            q_across(i)

    @pl.when(jnp.logical_not(first))
    def _():
        for i in (3, 7, 4, 5, 6):
            from_paired(i)

    @pl.when(first)
    def _():
        from_partner()

    other_pass(1)
    begin(weight_sent(1))
    begin(rc(tokens.at[rows(half * pe, half), :], tb.at[e], "t", 0, partner))
    pl.when(r == S - 1)(lambda: pl.semaphore_wait(ready.at[2], 1))
    pl.when(r == 0)(lambda: pl.semaphore_wait(ready.at[3], 1))
    for d in range(1, S):
        begin(rc(tab, tabr.at[d], "tab", d, zdev(d)))
    other_pass(2)

    for d in range(1, S):
        landed(tabr.at[d], "tab", d, zdev(d))
    places = tabr[0]
    for d in range(1, S):
        places = places + tabr[d]
    lidx_v[...] = places
    place_copy = pltpu.make_async_copy(lidx_v, lidx, lsem.at[C + 4])
    place_copy.start()
    pack_copy.wait()
    place_copy.wait()

    def z_copy(u, d):
        dst = zpeer(d)
        return rc(zs.at[u, dst], zr.at[u // 2, half_of(u), r], "z", u * S + d, zdev(d))

    def z_landed(u, d):
        source = zpeer(d)
        side = lax.rem(u + lax.rem(source, 2), 2)
        landed(zr.at[u // 2, side, source], "z", u * S + d, {"seq": source})

    def ctx_rows(side, c):
        return rows(CROWS * C * side + CROWS * c, CROWS)

    def own_rows(side, c):
        return ctx.at[:, pl.ds(2, NB_SEQ), ctx_rows(side, c), :]

    def forward_copy(c):
        return rc(own_rows(e, c), own_rows(e, c), "fwd", c, partner)

    def prior_copy(c, same_core):
        return rc(
            ctx.at[:, pl.ds(NB_SEQ, 2), ctx_rows(e, c), :],
            ctx.at[:, pl.ds(0, 2), ctx_rows(e, c), :],
            "pr0" if same_core else "pr1", c if same_core else 0,
            {"seq": lax.rem(r + 1, S), "enc": e if same_core else pe},
        )

    def encode(u):
        landed(str_.at[u], "st", u, across)
        landed(precv.at[u], "s", u, across)
        c = u // 2
        side = half_of(u)
        other = decoded(precv[u], as_column(str_[u, 0:LINES, :]))
        lined = ss[c, 0:LINES, :] + str_[u, LINES : 2 * LINES, :]
        factor = lax.rsqrt(as_column(lined) / D + epsilon)
        scaled = (sown[c, :, lanes(side)] + other) * factor
        enc[u] = scaled.astype(jnp.bfloat16).reshape(E, CROWS, 128)
        for d in (3, 2, 1, 0):
            dst = zpeer(d)
            for k in range(cap):
                block = enc[u, pidx[0, dst * cap + k]]
                if d:
                    zs[u, dst, k] = block
                else:
                    zr[c, side, r, k] = block
            if d:
                z_copy(u, d).start()

    def prior_forward(c):
        area = ctx.at[:, pl.ds(0, 2), ctx_rows(e, c), :]
        return rc(area, area, "pf", c, partner)

    def prior_on(c):
        landed(ctx.at[:, pl.ds(0, 2), ctx_rows(e, c), :], "pr0", c, below)
        prior_forward(c).start()

    def drain_units(u):
        partial_copy(u).wait_send()
        stat_copy(u).wait_send()
        for d in range(1, S):
            z_copy(u, d).wait_send()

    def place(c, last):
        for j in range(2):
            for d in range(1, S):
                z_landed(2 * c + j, d)
        zl[...] = zr[c].reshape(zl.shape)

        def put(l):
            where = lidx[0, r * NB_SEQ + l]
            ctx[0, 2 + l, ctx_rows(e, c), :] = zl[0, where]
            ctx[1, 2 + l, ctx_rows(e, c), :] = zl[1, where]

        put(NB_SEQ - 1)
        put(NB_SEQ - 2)

        @pl.when(r < S - 1)
        def _():
            prior_copy(c, True).start()
            if last:
                prior_copy(c, False).start()

        for l in range(NB_SEQ - 2):
            put(l)

        forward_copy(c).start()
        pl.when(jnp.logical_and(r > 0, c > 0))(lambda: prior_on(c - 1))

    TL = half // 128
    token_copy = rc(tsend, trecv, "ts", 0, across)
    token_stat = rc(st.at[2 * C], str_.at[2 * C], "st", 2 * C, across)

    def token_pass():
        for i in range(8):
            landed(qpiece(i, pe), "qe", i, partner)
        words, peak = coded(product(tb[0], tb[1], woq))
        st[2 * C, 0:TL, :] = as_rows(peak)
        st[2 * C, TL : 2 * TL, :] = ss[C, 0:TL, :]
        token_stat.start()
        tsend[...] = words
        token_copy.start()

    encode(0)
    other_pass(3)
    local_t.wait()
    landed(tb.at[pe], "t", 0, partner)
    local_q.wait()
    landed(wown.at[1, :, lanes(pe)], "wo", 1, partner)
    ss[C, 0:TL, :] = as_rows(squares(tb[0]) + squares(tb[1]))
    town[...] = product(tb[0], tb[1], wown.at[1])
    @pl.when(jnp.logical_not(first))
    def _():
        for i in range(4):
            q_paired(i)

    encode(1)
    pl.when(first)(lambda: q_beside(0))

    def middle(c, carry):
        @pl.when(c < C - 1)
        def _():
            own_pass(c + 1)
            other_pass(2 * c + 2)
            other_pass(2 * c + 3)

        @pl.when(jnp.logical_and(c == C - 1, jnp.logical_not(first)))
        def _():
            for i in range(4, 8):
                q_paired(i)

        @pl.when(c == C - 1)
        def _():
            token_pass()

        encode(2 * c)
        pl.when(jnp.logical_and(c == 1, first))(lambda: q_beside(1))
        pl.when(jnp.logical_and(c == 2, first))(lambda: q_beside(3))
        encode(2 * c + 1)
        pl.when(jnp.logical_and(c == 1, first))(lambda: q_beside(2))
        place(c - 1, False)
        drain_units(2 * c - 2)
        drain_units(2 * c - 1)
        return carry

    lax.fori_loop(1, C, middle, 0)

    landed(str_.at[2 * C], "st", 2 * C, across)
    landed(trecv, "ts", 0, across)
    lined = ss[C, 0:TL, :] + str_[2 * C, TL : 2 * TL, :]
    factor = lax.rsqrt(as_column(lined) / D + epsilon) * 128 ** (-0.5)
    scaled = (town[...] + decoded(trecv[...], as_column(str_[2 * C, 0:TL, :]))) * factor
    rounded = scaled.astype(jnp.bfloat16)
    low = e == 0
    qb[e] = jnp.where(low, rounded[:, :128], rounded[:, 128:])
    qs[...] = jnp.where(low, rounded[:, 128:], rounded[:, :128])
    begin(rc(qs, qb.at[e], "q", 0, partner))

    place(C - 1, True)
    landed(qb.at[pe], "q", 0, partner)

    def settle(c, carry):
        landed(own_rows(pe, c), "fwd", c, partner)
        return carry

    lax.fori_loop(0, C, settle, 0)

    spans = half // SPAN

    def attend(those):
        scores = []
        for c in those:
            queries = qb[c // spans, rows(c % spans * SPAN, SPAN), :]
            keys = ctx[0, pl.ds(2 * c, 2)].reshape(NBR * RLEN, 128)
            scores.append(
                lax.dot_general(
                    queries, keys, (((1,), (1,)), ((), ())), preferred_element_type=f32
                )
            )
        raised = [jnp.exp(s - jnp.max(s, axis=1, keepdims=True)) for s in scores]
        weight = [(x / jnp.sum(x, axis=1, keepdims=True)).astype(jnp.bfloat16) for x in raised]
        for c, w in zip(those, weight):
            values = ctx[1, pl.ds(2 * c, 2)].reshape(NBR * RLEN, 128)
            mixed = jnp.dot(w, values, preferred_element_type=f32)
            out[rows(c * SPAN, SPAN), :] = mixed.astype(jnp.bfloat16)

    attend(range(1, 2 * spans))

    def settle_prior(c, carry):
        @pl.when(r > 0)
        def _():
            landed(ctx.at[:, pl.ds(0, 2), ctx_rows(pe, c), :], "pf", c, partner)

        return carry

    lax.fori_loop(0, C - 1, settle_prior, 0)

    @pl.when(r > 0)
    def _():
        landed(ctx.at[:, pl.ds(0, 2), ctx_rows(e, C - 1), :], "pr0", C - 1, below)
        across_core = {"seq": lax.rem(r + S - 1, S), "enc": pe}
        landed(ctx.at[:, pl.ds(0, 2), ctx_rows(pe, C - 1), :], "pr1", 0, across_core)

    attend([0])

    def drain(c, carry):
        sent_chunk(c).wait_send()
        forward_copy(c).wait_send()
        pl.when(r < S - 1)(lambda: prior_copy(c, True).wait_send())
        pl.when(jnp.logical_and(r > 0, c < C - 1))(lambda: prior_forward(c).wait_send())
        return carry

    lax.fori_loop(0, C, drain, 0)
    pl.when(r < S - 1)(lambda: prior_copy(C - 1, False).wait_send())
    drain_units(2 * C - 2)
    drain_units(2 * C - 1)
    token_copy.wait_send()
    token_stat.wait_send()
    for i in range(8):
        ke(i).wait_send()
        qstep("qe", i, partner).wait_send()

    @pl.when(first)
    def _():
        for i in (0, 1, 2, 3, 7):
            kx(i).wait_send()
        for i in range(3):
            ky(i).wait_send()
        for i in range(8):
            kz(i).wait_send()
            qstep("qz", i, paired).wait_send()
        for i in range(4):
            qx(i).wait_send()
            qstep("qy", i, beside).wait_send()

    for copy in done:
        copy.wait_send()


def SEMAPHORES(S):
    C = CHUNKS
    return (
        ("kx", 8), ("ky", 3), ("kz", 8), ("ke", 8), ("wo", 2), ("qx", 4), ("qy", 4), ("qz", 8), ("qe", 8),
        ("x", C), ("t", 1), ("s", 2 * C), ("st", 2 * C + 1), ("ts", 1), ("tab", S), ("z", 2 * C * S),
        ("fwd", C), ("pr0", C), ("pr1", 1), ("pf", C), ("q", 1),
    )


def local_fused(tokens, nbr_feats, counts, slot_target, w_query, w_keyval):
    S = lax.axis_size("seq")
    cap = max(2, 2 * NB_SEQ // S)
    K = tokens.shape[1]
    half = tokens.shape[0] // 2
    C = CHUNKS
    bf, f32, i32 = jnp.bfloat16, jnp.float32, jnp.int32
    anywhere = pl.BlockSpec(memory_space=pl.ANY)
    vmem = pl.BlockSpec(memory_space=pltpu.VMEM)
    count = sum(size for _, size in SEMAPHORES(S))
    return pl.pallas_call(
        functools.partial(fused, S, cap),
        out_shape=jax.ShapeDtypeStruct((2 * half, 128), bf),
        in_specs=[vmem, vmem] + [anywhere] * 4,
        out_specs=vmem,
        scratch_shapes=[
            pltpu.VMEM((2, C, ENC_CAP, CROWS, K), bf),
            pltpu.VMEM((2, half, K), bf),
            pltpu.VMEM((2, 2 * K, 256), bf),
            pltpu.VMEM((2, 2 * K, 128), bf),
            pltpu.VMEM((2 * K, 256), bf),
            pltpu.VMEM((C, CFLAT, 256), f32),
            pltpu.VMEM((2 * C, CFLAT * 3 // 4, 128), i32),
            pltpu.VMEM((2 * C, CFLAT * 3 // 4, 128), i32),
            pltpu.VMEM((half, 256), f32),
            pltpu.VMEM((half * 3 // 4, 256), i32),
            pltpu.VMEM((half * 3 // 4, 256), i32),
            pltpu.VMEM((C + 1, 8, 128), f32),
            pltpu.VMEM((2 * C + 1, 8, 128), f32),
            pltpu.VMEM((2 * C + 1, 8, 128), f32),
            pltpu.VMEM((2 * C, ENC_CAP, CROWS, 128), bf),
            pltpu.VMEM((2 * C, S, cap, CROWS, 128), bf),
            pltpu.VMEM((C, 2, S, cap, CROWS, 128), bf),
            pltpu.VMEM((2, S * cap, CROWS, 128), bf),
            pltpu.VMEM((2, NB_SEQ + 2, RLEN, 128), bf),
            pltpu.VMEM((2, half, 128), bf),
            pltpu.VMEM((half, 128), bf),
            pltpu.VMEM((8, 128), i32),
            pltpu.VMEM((S, 8, 128), i32),
            pltpu.VMEM((8, 128), i32),
            pltpu.VMEM((8, 128), i32),
            pltpu.SMEM((8, 128), i32),
            pltpu.SMEM((8, 128), i32),
            pltpu.SemaphoreType.DMA((C + 5,)),
            pltpu.SemaphoreType.DMA((count,)),
            pltpu.SemaphoreType.DMA((count,)),
            pltpu.SemaphoreType.REGULAR((4,)),
        ],
        compiler_params=pltpu.CompilerParams(
            collective_id=0, has_side_effects=True, vmem_limit_bytes=56 << 20
        ),
    )(slot_target.reshape(1, -1), counts.reshape(1, -1), nbr_feats, tokens, w_query, w_keyval)


def solution(mesh):
    small = mesh.shape["mp"] == 2 and mesh.shape["groups"] == 2 and mesh.shape["seq"] == 4
    placed = (
        P(("groups", "seq"), ("mp", "enc")),
        P(("groups", "seq"), None, ("mp", "enc")),
        P("groups"),
        P(("groups", "seq")),
        P(None, ("mp", "enc")),
        P(None, ("mp", "enc")),
    )
    return jax.shard_map(
        local_fused if small else local,
        mesh=mesh,
        in_specs=placed,
        out_specs=P(("groups", "seq"), ("mp", "enc")),
        check_vma=False,
    )
```

```python
import functools
import jax
import jax.numpy as jnp
from jax import lax
from jax.experimental import pallas as pl
from jax.experimental.pallas import tpu as pltpu
from jax.sharding import PartitionSpec as P

D = 4096
SPAN = 64
NBR = 2
RLEN = 128
CH_SEQ = 8
NB_SEQ = 16
ENC_CAP = 24


epsilon = 1e-05


def partner_2(block, axis, stride):
    count = lax.axis_size(axis)
    route = []
    for low in range(count):
        high = low | 1 << stride
        if high != low and high < count:
            route += [(low, high), (high, low)]
    return lax.ppermute(block, axis, route)


def passed_along(block, axis, distance):
    devices = range(lax.axis_size(axis))
    route = [(i - distance, i) for i in devices if i - distance in devices]
    return lax.ppermute(block, axis, route)


def project_fold(weight, piece):
    width = piece.shape[-1]
    flat_rows = piece.reshape(-1, width)
    mine = lax.all_to_all(weight, ("mp", "enc"), split_axis=0, concat_axis=1, tiled=True)
    partial = jnp.dot(flat_rows, mine, preferred_element_type=jnp.float32)
    running = lax.psum_scatter(partial, ("mp", "enc"), scatter_dimension=1, tiled=True)
    widened = flat_rows.astype(jnp.float32)
    squares = lax.psum(jnp.sum(widened * widened, axis=1), ("mp", "enc"))
    return (running, squares)


def normalized(carry, factor):
    running, squares = carry
    scale_rows = lax.rsqrt(squares / D + epsilon) * factor
    return (running * scale_rows[:, None]).astype(jnp.bfloat16)


def routing_plan(slot_target, counts, pair_cap):
    seq_count = counts.shape[0]
    seq_here = lax.axis_index("seq")
    live_count = jnp.sum(jnp.where(jnp.arange(seq_count) == seq_here, counts, 0))
    slot_ids = jnp.arange(ENC_CAP)
    live_slots = slot_ids < live_count
    owner_of = slot_target // NB_SEQ
    position = slot_target % NB_SEQ
    same_owner = (
        (owner_of[:, None] == owner_of[None, :])
        & live_slots[None, :]
        & (slot_ids[None, :] < slot_ids[:, None])
    )
    rank_within = jnp.sum(same_owner.astype(jnp.int32), axis=1)
    target_slot = owner_of * pair_cap + rank_within
    buffer_ids = jnp.arange(seq_count * pair_cap)
    chosen = (buffer_ids[:, None] == target_slot[None, :]) & live_slots[None, :]
    sent_ids = jnp.sum(jnp.where(chosen, position[None, :] + 1, 0), axis=1) - 1
    return (chosen, sent_ids.reshape(seq_count, pair_cap))


def pack_rows(chosen, payload, seq_count, pair_cap):
    packed = jnp.dot(chosen.astype(jnp.bfloat16), payload, preferred_element_type=jnp.float32)
    return packed.astype(jnp.bfloat16).reshape(seq_count, pair_cap, payload.shape[1])


def place_rows(received, received_ids):
    flat_rows = received.reshape(-1, received.shape[-1])
    picker = received_ids.reshape(1, -1) == jnp.arange(NB_SEQ)[:, None]
    placed = jnp.dot(picker.astype(jnp.bfloat16), flat_rows, preferred_element_type=jnp.float32)
    return placed.astype(jnp.bfloat16)


def local(tokens, nbr_feats, counts, slot_target, w_query, w_keyval):
    seq_count = lax.axis_size("seq")
    pair_cap = max(2, 2 * NB_SEQ // seq_count)
    head_size = w_keyval.shape[1]
    chosen, sent_ids = routing_plan(slot_target, counts, pair_cap)
    folded = project_fold(w_keyval, nbr_feats)
    encoded = normalized(folded, 1.0).reshape(ENC_CAP, RLEN * head_size)
    packed = pack_rows(chosen, encoded, seq_count, pair_cap)
    received, received_ids = (
        lax.all_to_all(packed, "seq", split_axis=0, concat_axis=0, tiled=True),
        lax.all_to_all(sent_ids, "seq", split_axis=0, concat_axis=0, tiled=True),
    )
    own_half = place_rows(received, received_ids).reshape(NB_SEQ, RLEN, head_size)
    partner = partner_2(own_half, "enc", 0)
    first_lane = lax.axis_index("enc") == 0
    key_rows = jnp.where(first_lane, own_half, partner).reshape(CH_SEQ, NBR * RLEN, head_size)
    value_rows = jnp.where(first_lane, partner, own_half).reshape(CH_SEQ, NBR * RLEN, head_size)
    prior_keys, prior_values = passed_along((key_rows[-1], value_rows[-1]), "seq", 1)
    context_keys = jnp.concatenate([prior_keys[None], key_rows[:-1]], axis=0)
    context_values = jnp.concatenate([prior_values[None], value_rows[:-1]], axis=0)
    folded_tokens = project_fold(w_query, tokens)
    queries = normalized(folded_tokens, head_size ** (-0.5)).reshape(CH_SEQ, SPAN, head_size)
    scores = jnp.einsum("cqd,ckd->cqk", queries, context_keys, preferred_element_type=jnp.float32)
    weights = jax.nn.softmax(scores, axis=-1).astype(jnp.bfloat16)
    attended = jnp.einsum(
        "cqk,ckd->cqd", weights, context_values, preferred_element_type=jnp.float32
    )
    return attended.astype(jnp.bfloat16).reshape(CH_SEQ * SPAN, head_size)


CHUNKS = 4
CROWS = RLEN // 2 // CHUNKS
CFLAT = ENC_CAP * CROWS
LINES = CFLAT // 128
KV_BITS = 22
KV_WORDS = CFLAT * KV_BITS // 32


def fused(
    S, cap, trow, cnt, feats, tokens, wq, wkv, out,
    xb, tb, wown, wo, woq, sown, psend, precv, town, tsend, trecv, ss, st, str_,
    enc, zs, zr, zl, ctx, qb, qs, tab, tabr, pidx_v, lidx_v, pidx, lidx,
    lsem, send, recv, ready,
):
    f32, i32 = jnp.float32, jnp.int32
    g, r, m, e = (lax.axis_index(a) for a in ("groups", "seq", "mp", "enc"))
    pg, pm, pe = 1 - g, 1 - m, 1 - e
    p = lax.rem(r, 2)
    first = e == p
    K = feats.shape[2]
    half = tokens.shape[0] // 2
    C = CHUNKS
    Q = K // 4
    partner, across, beside = {"enc": pe}, {"mp": pm}, {"groups": pg}
    paired = {"seq": r + 1 - 2 * p}

    ids = {}
    total = 0
    for name, count in SEMAPHORES(S):
        ids[name] = total
        total += count

    def rc(src, dst, name, at, device):
        i = ids[name] + at
        return pltpu.make_async_remote_copy(
            src_ref=src, dst_ref=dst, send_sem=send.at[i], recv_sem=recv.at[i],
            device_id=device, device_id_type=pl.DeviceIdType.MESH,
        )

    def landed(dst, name, at, device):
        rc(dst, dst, name, at, device).wait_recv()

    def lanes(index):
        return pl.ds(pl.multiple_of(index * 128, 128), 128)

    def rows(start, size):
        return pl.ds(pl.multiple_of(start, 16), size)

    def zpeer(d):
        return (r, r + 1 - 2 * p, lax.rem(r + 2, 4), 3 - r)[d]

    def zdev(d):
        return {"seq": zpeer(d)}

    done = []

    def begin(copy):
        copy.start()
        done.append(copy)

    barrier = pltpu.get_barrier_semaphore()
    above, below = {"seq": lax.rem(r + 1, S)}, {"seq": lax.rem(r + S - 1, S)}

    def signal(semaphore, device):
        pl.semaphore_signal(semaphore, inc=1, device_id=device, device_id_type=pl.DeviceIdType.MESH)

    for device in (across, beside, partner):
        signal(barrier, device)
    pl.when(r < S - 1)(lambda: signal(barrier, above))
    pl.when(r > 0)(lambda: signal(barrier, below))

    def kstart(i):
        return (K * g if i < 4 else K * pg) + i % 4 * Q

    def krow(i):
        return rows(kstart(i), Q)

    def kx(i):
        source = wkv.at[rows(2 * K * pm + kstart(i), Q), :]
        return rc(source, wo.at[e, krow(i)], "kx", i, across)

    def ky(i):
        return rc(wo.at[e, krow(i)], wo.at[e, krow(i)], "ky", i, beside)

    def kz(i):
        return rc(wo.at[e, krow(i)], wo.at[e, krow(i)], "kz", i, paired)

    def ke(i):
        return rc(wo.at[e, krow(i)], wo.at[e, krow(i)], "ke", i, partner)

    def from_across(i):
        landed(wo.at[e, krow(i)], "kx", i, across)
        if i < 3:
            ky(i).start()
        ke(i).start()
        kz(i).start()

    def from_beside(i):
        landed(wo.at[e, krow(4 + i)], "ky", i, beside)
        ke(4 + i).start()
        kz(4 + i).start()

    def from_paired(i):
        landed(wo.at[e, krow(i)], "kz", i, paired)
        ke(i).start()

    def from_partner():
        for i in range(8):
            landed(wo.at[pe, krow(i)], "ke", i, partner)

    def qpiece(i, side):
        start = (K * g if i < 4 else K * pg) + i % 4 * Q
        return woq.at[rows(start, Q), lanes(side)]

    def qx(i):
        source = wq.at[rows(2 * K * pm + K * g + i * Q, Q), :]
        return rc(source, qpiece(i, e), "qx", i, across)

    def qstep(name, i, device):
        return rc(qpiece(i, e), qpiece(i, e), name, i, device)

    def q_across(i):
        landed(qpiece(i, e), "qx", i, across)
        qstep("qy", i, beside).start()
        qstep("qe", i, partner).start()
        qstep("qz", i, paired).start()

    def q_beside(i):
        landed(qpiece(4 + i, e), "qy", i, beside)
        qstep("qe", 4 + i, partner).start()
        qstep("qz", 4 + i, paired).start()

    def q_paired(i):
        landed(qpiece(i, e), "qz", i, paired)
        qstep("qe", i, partner).start()

    weights = (wkv, wq)

    def weight_local(k):
        source = weights[k].at[rows(2 * K * m, 2 * K), :]
        return pltpu.make_async_copy(source, wown.at[k, :, lanes(e)], lsem.at[C + k])

    def weight_sent(k):
        source = weights[k].at[rows(2 * K * m, 2 * K), :]
        return rc(source, wown.at[k, :, lanes(e)], "wo", k, partner)

    def own_chunk(c):
        return pltpu.make_async_copy(
            feats.at[:, rows(CROWS * C * e + CROWS * c, CROWS), :], xb.at[e, c], lsem.at[c]
        )

    def sent_chunk(c):
        return rc(
            feats.at[:, rows(CROWS * C * pe + CROWS * c, CROWS), :], xb.at[e, c], "x", c, partner
        )

    local_kv = weight_local(0)
    local_kv.start()
    for c in range(C):
        own_chunk(c).start()
    local_q = weight_local(1)
    local_q.start()
    local_t = pltpu.make_async_copy(tokens.at[rows(half * e, half), :], tb.at[e], lsem.at[C + 2])
    local_t.start()

    pl.semaphore_wait(barrier, 3 + jnp.where(r > 0, 1, 0) + jnp.where(r < S - 1, 1, 0))

    @pl.when(jnp.logical_and(r > 0, r < S - 1))
    def _():
        signal(ready.at[0], above)
        signal(ready.at[1], below)

    @pl.when(first)
    def _():
        for i in (0, 1, 2, 3, 7):
            kx(i).start()
        for i in range(4):
            qx(i).start()

    begin(weight_sent(0))
    sent_chunk(0).start()
    sent_chunk(1).start()

    t_row = trow[...]
    iota = lambda shape, axis: lax.broadcasted_iota(jnp.int32, shape, axis)
    E = ENC_CAP
    t_col = jnp.sum(jnp.where(iota((E, E), 0) == iota((E, E), 1), t_row, 0), axis=1, keepdims=True)
    live = jnp.sum(jnp.where(iota((1, S), 1) == r, cnt[...], 0), axis=1, keepdims=True)
    same = (
        ((t_col >> 4) == (t_row >> 4)) & (iota((E, E), 1) < live) & (iota((E, E), 1) < iota((E, E), 0))
    )
    rank = jnp.sum(jnp.where(same, 1, 0), axis=1, keepdims=True)
    at_lane = iota((E, 128), 1)
    slot = iota((E, 128), 0)
    is_live = slot < live
    wanted = ((t_col >> 4) * cap + rank == at_lane) & is_live
    source_row = jnp.sum(jnp.where(wanted, slot, 0), axis=0, keepdims=True)
    held = (t_col == at_lane) & is_live
    place_row = jnp.sum(jnp.where(held, r * cap + rank, 0), axis=0, keepdims=True)
    pidx_v[...] = jnp.broadcast_to(source_row, (8, 128))
    tab[...] = jnp.broadcast_to(place_row, (8, 128))
    pack_copy = pltpu.make_async_copy(pidx_v, pidx, lsem.at[C + 3])
    pack_copy.start()
    tabr[0] = tab[...]
    ss[...] = jnp.zeros_like(ss)
    st[...] = jnp.zeros_like(st)

    @pl.when(r == 0)
    def _():
        ctx[:, 0:2] = jnp.zeros((2, 2) + ctx.shape[2:], ctx.dtype)

    eye = iota((128, 128), 0) == iota((128, 128), 1)

    def as_rows(column):
        blocks = column.reshape(-1, 128, 1)
        return jnp.sum(jnp.where(eye[None], blocks, 0.0), axis=1)

    def as_column(lined):
        blocks = jnp.where(eye[None], lined[:, None, :], 0.0)
        return jnp.sum(blocks, axis=2, keepdims=True).reshape(-1, 1)

    def squares(block):
        wide = block.astype(f32)
        return jnp.sum(wide * wide, axis=1, keepdims=True)

    def product(one, two, weight):
        return jnp.dot(one, weight[:K, :], preferred_element_type=f32) + jnp.dot(
            two, weight[K:, :], preferred_element_type=f32
        )

    def chunk_rows(c):
        return xb[0, c].reshape(CFLAT, K), xb[1, c].reshape(CFLAT, K)

    def own_pass(c):
        own_chunk(c).wait()
        landed(xb.at[pe, c], "x", c, partner)
        one, two = chunk_rows(c)
        ss[c, 0:LINES, :] = as_rows(squares(one) + squares(two))
        sown[c] = product(one, two, wown.at[0])

    def fields(bits):
        low = 32 - bits
        spare, width = [], {22: 11, 24: 3}[bits] * low
        at = 0
        while at < width:
            size = min(low - at % low, bits - at % bits)
            spare.append((at // low, at % low, at // bits, at % bits, (1 << size) - 1))
            at += size
        return low, {22: (11, 16), 24: (3, 4)}[bits], spare

    def coded(part, bits):
        low, (words, blocks), spare = fields(bits)
        top = float((1 << (bits - 1)) - 8)
        peak = jnp.maximum(jnp.max(jnp.abs(part), axis=1, keepdims=True), 1e-30)
        whole = jnp.floor(part * (top / peak) + 0.5).astype(i32)
        size = part.shape[0] // blocks
        block = [whole[i * size : (i + 1) * size] for i in range(blocks)]
        word = [b << low for b in block[:words]]
        for i, shift, other, start, mask in spare:
            word[i] = word[i] | (((block[words + other] >> start) & mask) << shift)
        return jnp.concatenate(word, axis=0), peak

    def decoded(coding, peak, bits):
        low, (words, blocks), spare = fields(bits)
        top = float((1 << (bits - 1)) - 8)
        size = coding.shape[0] // words
        word = [coding[i * size : (i + 1) * size] for i in range(words)]
        block = [w >> low for w in word] + [None] * (blocks - words)
        for i, shift, other, start, mask in spare:
            piece = ((word[i] >> shift) & mask) << start
            k = words + other
            block[k] = piece if block[k] is None else block[k] | piece
        for k in range(words, blocks):
            block[k] = (block[k] << low) >> low
        return jnp.concatenate(block, axis=0).astype(f32) * (peak * (1.0 / top))

    def half_of(u):
        return lax.rem(u + p, 2)

    def partial_copy(u):
        return rc(psend.at[u], precv.at[u], "s", u, across)

    def stat_copy(u):
        return rc(st.at[u], str_.at[u], "st", u, across)

    def other_pass(u):
        c = u // 2
        one, two = chunk_rows(c)
        words, peak = coded(product(one, two, wo.at[half_of(u)]), KV_BITS)
        st[u, 0:LINES, :] = as_rows(peak)
        st[u, LINES : 2 * LINES, :] = ss[c, 0:LINES, :]
        stat_copy(u).start()
        psend[u] = words
        partial_copy(u).start()

    @pl.when(first)
    def _():
        from_across(0)

    local_kv.wait()
    landed(wown.at[0, :, lanes(pe)], "wo", 0, partner)
    own_pass(0)

    @pl.when(r > 1)
    def _():
        pl.semaphore_wait(ready.at[0], 1)
        pl.when(r < S - 1)(lambda: signal(ready.at[2], above))

    @pl.when(r < S - 2)
    def _():
        pl.semaphore_wait(ready.at[1], 1)
        pl.when(r > 0)(lambda: signal(ready.at[3], below))

    @pl.when(first)
    def _():
        for i in range(1, 4):
            from_across(i)

    sent_chunk(2).start()
    own_pass(1)

    @pl.when(first)
    def _():
        from_across(7)
        for i in range(3):
            from_beside(i)

    @pl.when(jnp.logical_not(first))
    def _():
        for i in range(3):
            from_paired(i)
        from_partner()

    other_pass(0)
    sent_chunk(3).start()

    @pl.when(first)
    def _():
        for i in range(4):
            q_across(i)

    @pl.when(jnp.logical_not(first))
    def _():
        for i in (3, 7, 4, 5, 6):
            from_paired(i)

    @pl.when(first)
    def _():
        from_partner()

    other_pass(1)
    begin(weight_sent(1))
    begin(rc(tokens.at[rows(half * pe, half), :], tb.at[e], "t", 0, partner))
    pl.when(r == S - 1)(lambda: pl.semaphore_wait(ready.at[2], 1))
    pl.when(r == 0)(lambda: pl.semaphore_wait(ready.at[3], 1))
    for d in range(1, S):
        begin(rc(tab, tabr.at[d], "tab", d, zdev(d)))
    other_pass(2)

    for d in range(1, S):
        landed(tabr.at[d], "tab", d, zdev(d))
    places = tabr[0]
    for d in range(1, S):
        places = places + tabr[d]
    lidx_v[...] = places
    place_copy = pltpu.make_async_copy(lidx_v, lidx, lsem.at[C + 4])
    place_copy.start()
    pack_copy.wait()
    place_copy.wait()

    def z_copy(u, d):
        dst = zpeer(d)
        return rc(zs.at[u, dst], zr.at[u // 2, half_of(u), r], "z", u * S + d, zdev(d))

    def z_landed(u, d):
        source = zpeer(d)
        side = lax.rem(u + lax.rem(source, 2), 2)
        landed(zr.at[u // 2, side, source], "z", u * S + d, {"seq": source})

    def ctx_rows(side, c):
        return rows(CROWS * C * side + CROWS * c, CROWS)

    def own_rows(side, c):
        return ctx.at[:, pl.ds(2, NB_SEQ), ctx_rows(side, c), :]

    def forward_copy(c):
        return rc(own_rows(e, c), own_rows(e, c), "fwd", c, partner)

    def prior_copy(c, same_core):
        return rc(
            ctx.at[:, pl.ds(NB_SEQ, 2), ctx_rows(e, c), :],
            ctx.at[:, pl.ds(0, 2), ctx_rows(e, c), :],
            "pr0" if same_core else "pr1", c if same_core else 0,
            {"seq": lax.rem(r + 1, S), "enc": e if same_core else pe},
        )

    def encode(u):
        landed(str_.at[u], "st", u, across)
        landed(precv.at[u], "s", u, across)
        c = u // 2
        side = half_of(u)
        other = decoded(precv[u], as_column(str_[u, 0:LINES, :]), KV_BITS)
        lined = ss[c, 0:LINES, :] + str_[u, LINES : 2 * LINES, :]
        factor = lax.rsqrt(as_column(lined) / D + epsilon)
        scaled = (sown[c, :, lanes(side)] + other) * factor
        enc[u] = scaled.astype(jnp.bfloat16).reshape(E, CROWS, 128)
        for d in (3, 2, 1, 0):
            dst = zpeer(d)
            for k in range(cap):
                block = enc[u, pidx[0, dst * cap + k]]
                if d:
                    zs[u, dst, k] = block
                else:
                    zr[c, side, r, k] = block
            if d:
                z_copy(u, d).start()

    def prior_forward(c):
        area = ctx.at[:, pl.ds(0, 2), ctx_rows(e, c), :]
        return rc(area, area, "pf", c, partner)

    def prior_on(c):
        landed(ctx.at[:, pl.ds(0, 2), ctx_rows(e, c), :], "pr0", c, below)
        prior_forward(c).start()

    def drain_units(u):
        partial_copy(u).wait_send()
        stat_copy(u).wait_send()
        for d in range(1, S):
            z_copy(u, d).wait_send()

    def place(c, last):
        for j in range(2):
            for d in range(1, S):
                z_landed(2 * c + j, d)
        zl[...] = zr[c].reshape(zl.shape)

        def put(l):
            where = lidx[0, r * NB_SEQ + l]
            ctx[0, 2 + l, ctx_rows(e, c), :] = zl[0, where]
            ctx[1, 2 + l, ctx_rows(e, c), :] = zl[1, where]

        put(NB_SEQ - 1)
        put(NB_SEQ - 2)

        @pl.when(r < S - 1)
        def _():
            prior_copy(c, True).start()
            if last:
                prior_copy(c, False).start()

        for l in range(NB_SEQ - 2):
            put(l)

        forward_copy(c).start()
        pl.when(jnp.logical_and(r > 0, c > 0))(lambda: prior_on(c - 1))

    TL = half // 128
    token_copy = rc(tsend, trecv, "ts", 0, across)
    token_stat = rc(st.at[2 * C], str_.at[2 * C], "st", 2 * C, across)

    def token_pass():
        for i in range(8):
            landed(qpiece(i, pe), "qe", i, partner)
        words, peak = coded(product(tb[0], tb[1], woq), 24)
        st[2 * C, 0:TL, :] = as_rows(peak)
        st[2 * C, TL : 2 * TL, :] = ss[C, 0:TL, :]
        token_stat.start()
        tsend[...] = words
        token_copy.start()

    encode(0)
    other_pass(3)
    local_t.wait()
    landed(tb.at[pe], "t", 0, partner)
    local_q.wait()
    landed(wown.at[1, :, lanes(pe)], "wo", 1, partner)
    ss[C, 0:TL, :] = as_rows(squares(tb[0]) + squares(tb[1]))
    town[...] = product(tb[0], tb[1], wown.at[1])
    @pl.when(jnp.logical_not(first))
    def _():
        for i in range(4):
            q_paired(i)

    encode(1)
    pl.when(first)(lambda: q_beside(0))

    def middle(c, carry):
        @pl.when(c < C - 1)
        def _():
            own_pass(c + 1)
            other_pass(2 * c + 2)
            other_pass(2 * c + 3)

        @pl.when(jnp.logical_and(c == C - 1, jnp.logical_not(first)))
        def _():
            for i in range(4, 8):
                q_paired(i)

        @pl.when(c == C - 1)
        def _():
            token_pass()

        encode(2 * c)
        pl.when(jnp.logical_and(c == 1, first))(lambda: q_beside(1))
        pl.when(jnp.logical_and(c == 2, first))(lambda: q_beside(3))
        encode(2 * c + 1)
        pl.when(jnp.logical_and(c == 1, first))(lambda: q_beside(2))
        place(c - 1, False)
        drain_units(2 * c - 2)
        drain_units(2 * c - 1)
        return carry

    lax.fori_loop(1, C, middle, 0)

    landed(str_.at[2 * C], "st", 2 * C, across)
    landed(trecv, "ts", 0, across)
    lined = ss[C, 0:TL, :] + str_[2 * C, TL : 2 * TL, :]
    factor = lax.rsqrt(as_column(lined) / D + epsilon) * 128 ** (-0.5)
    scaled = (town[...] + decoded(trecv[...], as_column(str_[2 * C, 0:TL, :]), 24)) * factor
    rounded = scaled.astype(jnp.bfloat16)
    low = e == 0
    qb[e] = jnp.where(low, rounded[:, :128], rounded[:, 128:])
    qs[...] = jnp.where(low, rounded[:, 128:], rounded[:, :128])
    token_query = rc(qs, qb.at[e], "q", 0, partner)
    token_query.start()

    def drain(c, carry):
        sent_chunk(c).wait_send()

        @pl.when(c < C - 1)
        def _():
            forward_copy(c).wait_send()
            pl.when(r < S - 1)(lambda: prior_copy(c, True).wait_send())

        pl.when(jnp.logical_and(r > 0, c < C - 2))(lambda: prior_forward(c).wait_send())
        return carry

    lax.fori_loop(0, C, drain, 0)
    drain_units(2 * C - 2)
    token_copy.wait_send()
    token_stat.wait_send()
    for i in range(8):
        ke(i).wait_send()
        qstep("qe", i, partner).wait_send()

    @pl.when(first)
    def _():
        for i in (0, 1, 2, 3, 7):
            kx(i).wait_send()
        for i in range(3):
            ky(i).wait_send()
        for i in range(8):
            kz(i).wait_send()
            qstep("qz", i, paired).wait_send()
        for i in range(4):
            qx(i).wait_send()
            qstep("qy", i, beside).wait_send()

    for copy in done:
        copy.wait_send()
    place(C - 1, True)
    drain_units(2 * C - 1)
    landed(qb.at[pe], "q", 0, partner)

    def settle(c, carry):
        landed(own_rows(pe, c), "fwd", c, partner)
        return carry

    lax.fori_loop(0, C, settle, 0)

    spans = half // SPAN

    def attend(those):
        scores = []
        for c in those:
            queries = qb[c // spans, rows(c % spans * SPAN, SPAN), :]
            keys = ctx[0, pl.ds(2 * c, 2)].reshape(NBR * RLEN, 128)
            scores.append(
                lax.dot_general(
                    queries, keys, (((1,), (1,)), ((), ())), preferred_element_type=f32
                )
            )
        raised = [jnp.exp(s - jnp.max(s, axis=1, keepdims=True)) for s in scores]
        weight = [(x / jnp.sum(x, axis=1, keepdims=True)).astype(jnp.bfloat16) for x in raised]
        for c, w in zip(those, weight):
            values = ctx[1, pl.ds(2 * c, 2)].reshape(NBR * RLEN, 128)
            mixed = jnp.dot(w, values, preferred_element_type=f32)
            out[rows(c * SPAN, SPAN), :] = mixed.astype(jnp.bfloat16)

    attend(range(1, 2 * spans))

    def settle_prior(c, carry):
        @pl.when(r > 0)
        def _():
            landed(ctx.at[:, pl.ds(0, 2), ctx_rows(pe, c), :], "pf", c, partner)

        return carry

    lax.fori_loop(0, C - 1, settle_prior, 0)

    @pl.when(r > 0)
    def _():
        landed(ctx.at[:, pl.ds(0, 2), ctx_rows(e, C - 1), :], "pr0", C - 1, below)
        across_core = {"seq": lax.rem(r + S - 1, S), "enc": pe}
        landed(ctx.at[:, pl.ds(0, 2), ctx_rows(pe, C - 1), :], "pr1", 0, across_core)

    attend([0])

    forward_copy(C - 1).wait_send()

    @pl.when(r < S - 1)
    def _():
        prior_copy(C - 1, True).wait_send()
        prior_copy(C - 1, False).wait_send()

    pl.when(r > 0)(lambda: prior_forward(C - 2).wait_send())
    token_query.wait_send()


def SEMAPHORES(S):
    C = CHUNKS
    return (
        ("kx", 8), ("ky", 3), ("kz", 8), ("ke", 8), ("wo", 2), ("qx", 4), ("qy", 4), ("qz", 8), ("qe", 8),
        ("x", C), ("t", 1), ("s", 2 * C), ("st", 2 * C + 1), ("ts", 1), ("tab", S), ("z", 2 * C * S),
        ("fwd", C), ("pr0", C), ("pr1", 1), ("pf", C), ("q", 1),
    )


def local_fused(tokens, nbr_feats, counts, slot_target, w_query, w_keyval):
    S = lax.axis_size("seq")
    cap = max(2, 2 * NB_SEQ // S)
    K = tokens.shape[1]
    half = tokens.shape[0] // 2
    C = CHUNKS
    bf, f32, i32 = jnp.bfloat16, jnp.float32, jnp.int32
    anywhere = pl.BlockSpec(memory_space=pl.ANY)
    vmem = pl.BlockSpec(memory_space=pltpu.VMEM)
    count = sum(size for _, size in SEMAPHORES(S))
    return pl.pallas_call(
        functools.partial(fused, S, cap),
        out_shape=jax.ShapeDtypeStruct((2 * half, 128), bf),
        in_specs=[vmem, vmem] + [anywhere] * 4,
        out_specs=vmem,
        scratch_shapes=[
            pltpu.VMEM((2, C, ENC_CAP, CROWS, K), bf),
            pltpu.VMEM((2, half, K), bf),
            pltpu.VMEM((2, 2 * K, 256), bf),
            pltpu.VMEM((2, 2 * K, 128), bf),
            pltpu.VMEM((2 * K, 256), bf),
            pltpu.VMEM((C, CFLAT, 256), f32),
            pltpu.VMEM((2 * C, KV_WORDS, 128), i32),
            pltpu.VMEM((2 * C, KV_WORDS, 128), i32),
            pltpu.VMEM((half, 256), f32),
            pltpu.VMEM((half * 3 // 4, 256), i32),
            pltpu.VMEM((half * 3 // 4, 256), i32),
            pltpu.VMEM((C + 1, 8, 128), f32),
            pltpu.VMEM((2 * C + 1, 8, 128), f32),
            pltpu.VMEM((2 * C + 1, 8, 128), f32),
            pltpu.VMEM((2 * C, ENC_CAP, CROWS, 128), bf),
            pltpu.VMEM((2 * C, S, cap, CROWS, 128), bf),
            pltpu.VMEM((C, 2, S, cap, CROWS, 128), bf),
            pltpu.VMEM((2, S * cap, CROWS, 128), bf),
            pltpu.VMEM((2, NB_SEQ + 2, RLEN, 128), bf),
            pltpu.VMEM((2, half, 128), bf),
            pltpu.VMEM((half, 128), bf),
            pltpu.VMEM((8, 128), i32),
            pltpu.VMEM((S, 8, 128), i32),
            pltpu.VMEM((8, 128), i32),
            pltpu.VMEM((8, 128), i32),
            pltpu.SMEM((8, 128), i32),
            pltpu.SMEM((8, 128), i32),
            pltpu.SemaphoreType.DMA((C + 5,)),
            pltpu.SemaphoreType.DMA((count,)),
            pltpu.SemaphoreType.DMA((count,)),
            pltpu.SemaphoreType.REGULAR((4,)),
        ],
        compiler_params=pltpu.CompilerParams(
            collective_id=0, has_side_effects=True, vmem_limit_bytes=56 << 20
        ),
    )(slot_target.reshape(1, -1), counts.reshape(1, -1), nbr_feats, tokens, w_query, w_keyval)


def solution(mesh):
    small = mesh.shape["mp"] == 2 and mesh.shape["groups"] == 2 and mesh.shape["seq"] == 4
    placed = (
        P(("groups", "seq"), ("mp", "enc")),
        P(("groups", "seq"), None, ("mp", "enc")),
        P("groups"),
        P(("groups", "seq")),
        P(None, ("mp", "enc")),
        P(None, ("mp", "enc")),
    )
    return jax.shard_map(
        local_fused if small else local,
        mesh=mesh,
        in_specs=placed,
        out_specs=P(("groups", "seq"), ("mp", "enc")),
        check_vma=False,
    )
```

```python
import functools
import jax
import jax.numpy as jnp
from jax import lax
from jax.experimental import pallas as pl
from jax.experimental.pallas import tpu as pltpu
from jax.sharding import PartitionSpec as P

D = 4096
SPAN = 64
NBR = 2
RLEN = 128
CH_SEQ = 8
NB_SEQ = 16
ENC_CAP = 24


epsilon = 1e-05


def partner_2(block, axis, stride):
    count = lax.axis_size(axis)
    route = []
    for low in range(count):
        high = low | 1 << stride
        if high != low and high < count:
            route += [(low, high), (high, low)]
    return lax.ppermute(block, axis, route)


def passed_along(block, axis, distance):
    devices = range(lax.axis_size(axis))
    route = [(i - distance, i) for i in devices if i - distance in devices]
    return lax.ppermute(block, axis, route)


def project_fold(weight, piece):
    width = piece.shape[-1]
    flat_rows = piece.reshape(-1, width)
    mine = lax.all_to_all(weight, ("mp", "enc"), split_axis=0, concat_axis=1, tiled=True)
    partial = jnp.dot(flat_rows, mine, preferred_element_type=jnp.float32)
    running = lax.psum_scatter(partial, ("mp", "enc"), scatter_dimension=1, tiled=True)
    widened = flat_rows.astype(jnp.float32)
    squares = lax.psum(jnp.sum(widened * widened, axis=1), ("mp", "enc"))
    return (running, squares)


def normalized(carry, factor):
    running, squares = carry
    scale_rows = lax.rsqrt(squares / D + epsilon) * factor
    return (running * scale_rows[:, None]).astype(jnp.bfloat16)


def routing_plan(slot_target, counts, pair_cap):
    seq_count = counts.shape[0]
    seq_here = lax.axis_index("seq")
    live_count = jnp.sum(jnp.where(jnp.arange(seq_count) == seq_here, counts, 0))
    slot_ids = jnp.arange(ENC_CAP)
    live_slots = slot_ids < live_count
    owner_of = slot_target // NB_SEQ
    position = slot_target % NB_SEQ
    same_owner = (
        (owner_of[:, None] == owner_of[None, :])
        & live_slots[None, :]
        & (slot_ids[None, :] < slot_ids[:, None])
    )
    rank_within = jnp.sum(same_owner.astype(jnp.int32), axis=1)
    target_slot = owner_of * pair_cap + rank_within
    buffer_ids = jnp.arange(seq_count * pair_cap)
    chosen = (buffer_ids[:, None] == target_slot[None, :]) & live_slots[None, :]
    sent_ids = jnp.sum(jnp.where(chosen, position[None, :] + 1, 0), axis=1) - 1
    return (chosen, sent_ids.reshape(seq_count, pair_cap))


def pack_rows(chosen, payload, seq_count, pair_cap):
    packed = jnp.dot(chosen.astype(jnp.bfloat16), payload, preferred_element_type=jnp.float32)
    return packed.astype(jnp.bfloat16).reshape(seq_count, pair_cap, payload.shape[1])


def place_rows(received, received_ids):
    flat_rows = received.reshape(-1, received.shape[-1])
    picker = received_ids.reshape(1, -1) == jnp.arange(NB_SEQ)[:, None]
    placed = jnp.dot(picker.astype(jnp.bfloat16), flat_rows, preferred_element_type=jnp.float32)
    return placed.astype(jnp.bfloat16)


def local(tokens, nbr_feats, counts, slot_target, w_query, w_keyval):
    seq_count = lax.axis_size("seq")
    pair_cap = max(2, 2 * NB_SEQ // seq_count)
    head_size = w_keyval.shape[1]
    chosen, sent_ids = routing_plan(slot_target, counts, pair_cap)
    folded = project_fold(w_keyval, nbr_feats)
    encoded = normalized(folded, 1.0).reshape(ENC_CAP, RLEN * head_size)
    packed = pack_rows(chosen, encoded, seq_count, pair_cap)
    received, received_ids = (
        lax.all_to_all(packed, "seq", split_axis=0, concat_axis=0, tiled=True),
        lax.all_to_all(sent_ids, "seq", split_axis=0, concat_axis=0, tiled=True),
    )
    own_half = place_rows(received, received_ids).reshape(NB_SEQ, RLEN, head_size)
    partner = partner_2(own_half, "enc", 0)
    first_lane = lax.axis_index("enc") == 0
    key_rows = jnp.where(first_lane, own_half, partner).reshape(CH_SEQ, NBR * RLEN, head_size)
    value_rows = jnp.where(first_lane, partner, own_half).reshape(CH_SEQ, NBR * RLEN, head_size)
    prior_keys, prior_values = passed_along((key_rows[-1], value_rows[-1]), "seq", 1)
    context_keys = jnp.concatenate([prior_keys[None], key_rows[:-1]], axis=0)
    context_values = jnp.concatenate([prior_values[None], value_rows[:-1]], axis=0)
    folded_tokens = project_fold(w_query, tokens)
    queries = normalized(folded_tokens, head_size ** (-0.5)).reshape(CH_SEQ, SPAN, head_size)
    scores = jnp.einsum("cqd,ckd->cqk", queries, context_keys, preferred_element_type=jnp.float32)
    weights = jax.nn.softmax(scores, axis=-1).astype(jnp.bfloat16)
    attended = jnp.einsum(
        "cqk,ckd->cqd", weights, context_values, preferred_element_type=jnp.float32
    )
    return attended.astype(jnp.bfloat16).reshape(CH_SEQ * SPAN, head_size)


CHUNKS = 4
CROWS = RLEN // 2 // CHUNKS
CFLAT = ENC_CAP * CROWS
LINES = CFLAT // 128
KV_BITS = 22
KV_WORDS = CFLAT * KV_BITS // 32


def fused(
    S, cap, trow, cnt, feats, tokens, wq, wkv, out,
    xb, tb, wown, wo, woq, sown, psend, precv, town, tsend, trecv, ss, st, str_,
    enc, zs, zr, zl, ctx, qb, qs, tab, tabr, pidx_v, lidx_v, pidx, lidx,
    lsem, send, recv, ready,
):
    f32, i32 = jnp.float32, jnp.int32
    g, r, m, e = (lax.axis_index(a) for a in ("groups", "seq", "mp", "enc"))
    pg, pm, pe = 1 - g, 1 - m, 1 - e
    p = lax.rem(r, 2)
    first = e == p
    K = feats.shape[2]
    half = tokens.shape[0] // 2
    C = CHUNKS
    Q = K // 4
    partner, across, beside = {"enc": pe}, {"mp": pm}, {"groups": pg}
    paired = {"seq": r + 1 - 2 * p}

    ids = {}
    total = 0
    for name, count in SEMAPHORES(S):
        ids[name] = total
        total += count

    def rc(src, dst, name, at, device):
        i = ids[name] + at
        return pltpu.make_async_remote_copy(
            src_ref=src, dst_ref=dst, send_sem=send.at[i], recv_sem=recv.at[i],
            device_id=device, device_id_type=pl.DeviceIdType.MESH,
        )

    def landed(dst, name, at, device):
        rc(dst, dst, name, at, device).wait_recv()

    def lanes(index):
        return pl.ds(pl.multiple_of(index * 128, 128), 128)

    def rows(start, size):
        return pl.ds(pl.multiple_of(start, 16), size)

    def zpeer(d):
        return (r, r + 1 - 2 * p, lax.rem(r + 2, 4), 3 - r)[d]

    def zdev(d):
        return {"seq": zpeer(d)}

    done = []

    def begin(copy):
        copy.start()
        done.append(copy)

    barrier = pltpu.get_barrier_semaphore()
    above, below = {"seq": lax.rem(r + 1, S)}, {"seq": lax.rem(r + S - 1, S)}

    def signal(semaphore, device):
        pl.semaphore_signal(semaphore, inc=1, device_id=device, device_id_type=pl.DeviceIdType.MESH)

    for device in (across, beside, partner):
        signal(barrier, device)
    pl.when(r < S - 1)(lambda: signal(barrier, above))
    pl.when(r > 0)(lambda: signal(barrier, below))

    def kstart(i):
        return (K * g if i < 4 else K * pg) + i % 4 * Q

    def krow(i):
        return rows(kstart(i), Q)

    def kx(i):
        source = wkv.at[rows(2 * K * pm + kstart(i), Q), :]
        return rc(source, wo.at[e, krow(i)], "kx", i, across)

    def ky(i):
        return rc(wo.at[e, krow(i)], wo.at[e, krow(i)], "ky", i, beside)

    def kz(i):
        return rc(wo.at[e, krow(i)], wo.at[e, krow(i)], "kz", i, paired)

    def ke(i):
        return rc(wo.at[e, krow(i)], wo.at[e, krow(i)], "ke", i, partner)

    def from_across(i):
        landed(wo.at[e, krow(i)], "kx", i, across)
        if i < 3:
            ky(i).start()
        ke(i).start()
        kz(i).start()

    def from_beside(i):
        landed(wo.at[e, krow(4 + i)], "ky", i, beside)
        ke(4 + i).start()
        kz(4 + i).start()

    def from_paired(i):
        landed(wo.at[e, krow(i)], "kz", i, paired)
        ke(i).start()

    def from_partner():
        for i in range(8):
            landed(wo.at[pe, krow(i)], "ke", i, partner)

    def qpiece(i, side):
        start = (K * g if i < 4 else K * pg) + i % 4 * Q
        return woq.at[rows(start, Q), lanes(side)]

    def qx(i):
        source = wq.at[rows(2 * K * pm + K * g + i * Q, Q), :]
        return rc(source, qpiece(i, e), "qx", i, across)

    def qstep(name, i, device):
        return rc(qpiece(i, e), qpiece(i, e), name, i, device)

    def q_across(i):
        landed(qpiece(i, e), "qx", i, across)
        qstep("qy", i, beside).start()
        qstep("qe", i, partner).start()
        qstep("qz", i, paired).start()

    def q_beside(i):
        landed(qpiece(4 + i, e), "qy", i, beside)
        qstep("qe", 4 + i, partner).start()
        qstep("qz", 4 + i, paired).start()

    def q_paired(i):
        landed(qpiece(i, e), "qz", i, paired)
        qstep("qe", i, partner).start()

    weights = (wkv, wq)

    def weight_local(k):
        source = weights[k].at[rows(2 * K * m, 2 * K), :]
        return pltpu.make_async_copy(source, wown.at[k, :, lanes(e)], lsem.at[C + k])

    def weight_sent(k):
        source = weights[k].at[rows(2 * K * m, 2 * K), :]
        return rc(source, wown.at[k, :, lanes(e)], "wo", k, partner)

    def own_chunk(c):
        return pltpu.make_async_copy(
            feats.at[:, rows(CROWS * C * e + CROWS * c, CROWS), :], xb.at[e, c], lsem.at[c]
        )

    def sent_chunk(c):
        return rc(
            feats.at[:, rows(CROWS * C * pe + CROWS * c, CROWS), :], xb.at[e, c], "x", c, partner
        )

    local_kv = weight_local(0)
    local_kv.start()
    for c in range(C):
        own_chunk(c).start()
    local_q = weight_local(1)
    local_q.start()
    local_t = pltpu.make_async_copy(tokens.at[rows(half * e, half), :], tb.at[e], lsem.at[C + 2])
    local_t.start()

    pl.semaphore_wait(barrier, 3 + jnp.where(r > 0, 1, 0) + jnp.where(r < S - 1, 1, 0))

    @pl.when(jnp.logical_and(r > 0, r < S - 1))
    def _():
        signal(ready.at[0], above)
        signal(ready.at[1], below)

    @pl.when(first)
    def _():
        for i in (0, 1, 2, 3, 7):
            kx(i).start()
        for i in range(4):
            qx(i).start()

    begin(weight_sent(0))
    sent_chunk(0).start()
    sent_chunk(1).start()

    t_row = trow[...]
    iota = lambda shape, axis: lax.broadcasted_iota(jnp.int32, shape, axis)
    E = ENC_CAP
    t_col = jnp.sum(jnp.where(iota((E, E), 0) == iota((E, E), 1), t_row, 0), axis=1, keepdims=True)
    live = jnp.sum(jnp.where(iota((1, S), 1) == r, cnt[...], 0), axis=1, keepdims=True)
    same = (
        ((t_col >> 4) == (t_row >> 4)) & (iota((E, E), 1) < live) & (iota((E, E), 1) < iota((E, E), 0))
    )
    rank = jnp.sum(jnp.where(same, 1, 0), axis=1, keepdims=True)
    at_lane = iota((E, 128), 1)
    slot = iota((E, 128), 0)
    is_live = slot < live
    wanted = ((t_col >> 4) * cap + rank == at_lane) & is_live
    source_row = jnp.sum(jnp.where(wanted, slot, 0), axis=0, keepdims=True)
    held = (t_col == at_lane) & is_live
    place_row = jnp.sum(jnp.where(held, r * cap + rank, 0), axis=0, keepdims=True)
    pidx_v[...] = jnp.broadcast_to(source_row, (8, 128))
    tab[...] = jnp.broadcast_to(place_row, (8, 128))
    pack_copy = pltpu.make_async_copy(pidx_v, pidx, lsem.at[C + 3])
    pack_copy.start()
    tabr[0] = tab[...]
    ss[...] = jnp.zeros_like(ss)
    st[...] = jnp.zeros_like(st)

    @pl.when(r == 0)
    def _():
        ctx[:, 0:2] = jnp.zeros((2, 2) + ctx.shape[2:], ctx.dtype)

    eye = iota((128, 128), 0) == iota((128, 128), 1)

    def as_rows(column):
        blocks = column.reshape(-1, 128, 1)
        return jnp.sum(jnp.where(eye[None], blocks, 0.0), axis=1)

    def as_column(lined):
        blocks = jnp.where(eye[None], lined[:, None, :], 0.0)
        return jnp.sum(blocks, axis=2, keepdims=True).reshape(-1, 1)

    def squares(block):
        wide = block.astype(f32)
        return jnp.sum(wide * wide, axis=1, keepdims=True)

    def product(one, two, weight):
        return jnp.dot(one, weight[:K, :], preferred_element_type=f32) + jnp.dot(
            two, weight[K:, :], preferred_element_type=f32
        )

    def chunk_rows(c):
        return xb[0, c].reshape(CFLAT, K), xb[1, c].reshape(CFLAT, K)

    def own_pass(c):
        own_chunk(c).wait()
        landed(xb.at[pe, c], "x", c, partner)
        one, two = chunk_rows(c)
        ss[c, 0:LINES, :] = as_rows(squares(one) + squares(two))
        sown[c] = product(one, two, wown.at[0])

    def fields(bits):
        low = 32 - bits
        spare, width = [], {22: 11, 24: 3}[bits] * low
        at = 0
        while at < width:
            size = min(low - at % low, bits - at % bits)
            spare.append((at // low, at % low, at // bits, at % bits, (1 << size) - 1))
            at += size
        return low, {22: (11, 16), 24: (3, 4)}[bits], spare

    def coded(part, bits):
        low, (words, blocks), spare = fields(bits)
        top = float((1 << (bits - 1)) - 8)
        peak = jnp.maximum(jnp.max(jnp.abs(part), axis=1, keepdims=True), 1e-30)
        whole = jnp.floor(part * (top / peak) + 0.5).astype(i32)
        size = part.shape[0] // blocks
        block = [whole[i * size : (i + 1) * size] for i in range(blocks)]
        word = [b << low for b in block[:words]]
        for i, shift, other, start, mask in spare:
            word[i] = word[i] | (((block[words + other] >> start) & mask) << shift)
        return jnp.concatenate(word, axis=0), peak

    def decoded(coding, peak, bits):
        low, (words, blocks), spare = fields(bits)
        top = float((1 << (bits - 1)) - 8)
        size = coding.shape[0] // words
        word = [coding[i * size : (i + 1) * size] for i in range(words)]
        block = [w >> low for w in word] + [None] * (blocks - words)
        for i, shift, other, start, mask in spare:
            piece = ((word[i] >> shift) & mask) << start
            k = words + other
            block[k] = piece if block[k] is None else block[k] | piece
        for k in range(words, blocks):
            block[k] = (block[k] << low) >> low
        return jnp.concatenate(block, axis=0).astype(f32) * (peak * (1.0 / top))

    def half_of(u):
        return lax.rem(u + p, 2)

    def partial_copy(u):
        return rc(psend.at[u], precv.at[u], "s", u, across)

    def stat_copy(u):
        return rc(st.at[u], str_.at[u], "st", u, across)

    def other_pass(u):
        c = u // 2
        one, two = chunk_rows(c)
        words, peak = coded(product(one, two, wo.at[half_of(u)]), KV_BITS)
        st[u, 0:LINES, :] = as_rows(peak)
        st[u, LINES : 2 * LINES, :] = ss[c, 0:LINES, :]
        stat_copy(u).start()
        psend[u] = words
        partial_copy(u).start()

    @pl.when(first)
    def _():
        from_across(0)

    local_kv.wait()
    landed(wown.at[0, :, lanes(pe)], "wo", 0, partner)
    own_pass(0)

    @pl.when(r > 1)
    def _():
        pl.semaphore_wait(ready.at[0], 1)
        pl.when(r < S - 1)(lambda: signal(ready.at[2], above))

    @pl.when(r < S - 2)
    def _():
        pl.semaphore_wait(ready.at[1], 1)
        pl.when(r > 0)(lambda: signal(ready.at[3], below))

    @pl.when(first)
    def _():
        for i in range(1, 4):
            from_across(i)

    sent_chunk(2).start()
    own_pass(1)

    @pl.when(first)
    def _():
        from_across(7)
        for i in range(3):
            from_beside(i)

    @pl.when(jnp.logical_not(first))
    def _():
        for i in range(3):
            from_paired(i)
        from_partner()

    other_pass(0)
    sent_chunk(3).start()

    @pl.when(first)
    def _():
        for i in range(4):
            q_across(i)

    @pl.when(jnp.logical_not(first))
    def _():
        for i in (3, 7, 4, 5, 6):
            from_paired(i)

    @pl.when(first)
    def _():
        from_partner()

    other_pass(1)
    begin(weight_sent(1))
    begin(rc(tokens.at[rows(half * pe, half), :], tb.at[e], "t", 0, partner))
    pl.when(r == S - 1)(lambda: pl.semaphore_wait(ready.at[2], 1))
    pl.when(r == 0)(lambda: pl.semaphore_wait(ready.at[3], 1))
    for d in range(1, S):
        begin(rc(tab, tabr.at[d], "tab", d, zdev(d)))
    other_pass(2)

    def z_copy(u, d):
        dst = zpeer(d)
        return rc(zs.at[u, dst], zr.at[u // 2, half_of(u), r], "z", u * S + d, zdev(d))

    def z_landed(u, d):
        source = zpeer(d)
        side = lax.rem(u + lax.rem(source, 2), 2)
        landed(zr.at[u // 2, side, source], "z", u * S + d, {"seq": source})

    def ctx_rows(side, c):
        return rows(CROWS * C * side + CROWS * c, CROWS)

    def own_rows(side, c):
        return ctx.at[:, pl.ds(2, NB_SEQ), ctx_rows(side, c), :]

    def forward_copy(c):
        return rc(own_rows(e, c), own_rows(e, c), "fwd", c, partner)

    def prior_copy(c, same_core):
        return rc(
            ctx.at[:, pl.ds(NB_SEQ, 2), ctx_rows(e, c), :],
            ctx.at[:, pl.ds(0, 2), ctx_rows(e, c), :],
            "pr0" if same_core else "pr1", c if same_core else 0,
            {"seq": lax.rem(r + 1, S), "enc": e if same_core else pe},
        )

    def encode(u):
        landed(str_.at[u], "st", u, across)
        landed(precv.at[u], "s", u, across)
        c = u // 2
        side = half_of(u)
        other = decoded(precv[u], as_column(str_[u, 0:LINES, :]), KV_BITS)
        lined = ss[c, 0:LINES, :] + str_[u, LINES : 2 * LINES, :]
        factor = lax.rsqrt(as_column(lined) / D + epsilon)
        scaled = (sown[c, :, lanes(side)] + other) * factor
        enc[u] = scaled.astype(jnp.bfloat16).reshape(E, CROWS, 128)
        for d in (3, 2, 1, 0):
            dst = zpeer(d)
            for k in range(cap):
                block = enc[u, pidx[0, dst * cap + k]]
                if d:
                    zs[u, dst, k] = block
                else:
                    zr[c, side, r, k] = block
            if d:
                z_copy(u, d).start()

    def prior_forward(c):
        area = ctx.at[:, pl.ds(0, 2), ctx_rows(e, c), :]
        return rc(area, area, "pf", c, partner)

    def prior_on(c):
        landed(ctx.at[:, pl.ds(0, 2), ctx_rows(e, c), :], "pr0", c, below)
        prior_forward(c).start()

    def drain_units(u):
        partial_copy(u).wait_send()
        stat_copy(u).wait_send()
        for d in range(1, S):
            z_copy(u, d).wait_send()

    def place(c, last):
        for j in range(2):
            for d in range(1, S):
                z_landed(2 * c + j, d)
        zl[...] = zr[c].reshape(zl.shape)

        def put(l):
            where = lidx[0, r * NB_SEQ + l]
            ctx[0, 2 + l, ctx_rows(e, c), :] = zl[0, where]
            ctx[1, 2 + l, ctx_rows(e, c), :] = zl[1, where]

        put(NB_SEQ - 1)
        put(NB_SEQ - 2)

        @pl.when(r < S - 1)
        def _():
            prior_copy(c, True).start()
            if last:
                prior_copy(c, False).start()

        for l in range(NB_SEQ - 2):
            put(l)

        forward_copy(c).start()
        pl.when(jnp.logical_and(r > 0, c > 0))(lambda: prior_on(c - 1))

    TL = half // 128
    token_copy = rc(tsend, trecv, "ts", 0, across)
    token_stat = rc(st.at[2 * C], str_.at[2 * C], "st", 2 * C, across)

    def token_pass():
        for i in range(8):
            landed(qpiece(i, pe), "qe", i, partner)
        words, peak = coded(product(tb[0], tb[1], woq), 24)
        st[2 * C, 0:TL, :] = as_rows(peak)
        st[2 * C, TL : 2 * TL, :] = ss[C, 0:TL, :]
        token_stat.start()
        tsend[...] = words
        token_copy.start()

    pack_copy.wait()
    encode(0)
    other_pass(3)
    local_t.wait()
    landed(tb.at[pe], "t", 0, partner)
    local_q.wait()
    landed(wown.at[1, :, lanes(pe)], "wo", 1, partner)
    ss[C, 0:TL, :] = as_rows(squares(tb[0]) + squares(tb[1]))
    town[...] = product(tb[0], tb[1], wown.at[1])
    @pl.when(jnp.logical_not(first))
    def _():
        for i in range(4):
            q_paired(i)

    encode(1)
    pl.when(first)(lambda: q_beside(0))
    for d in range(1, S):
        landed(tabr.at[d], "tab", d, zdev(d))
    places = tabr[0]
    for d in range(1, S):
        places = places + tabr[d]
    lidx_v[...] = places
    place_copy = pltpu.make_async_copy(lidx_v, lidx, lsem.at[C + 4])
    place_copy.start()
    place_copy.wait()

    def middle(c, carry):
        @pl.when(c < C - 1)
        def _():
            own_pass(c + 1)
            other_pass(2 * c + 2)
            other_pass(2 * c + 3)

        encode(2 * c)

        @pl.when(c == C - 1)
        def _():
            token_pass()

        pl.when(jnp.logical_and(c == 1, first))(lambda: q_beside(1))
        pl.when(jnp.logical_and(c == 2, first))(lambda: q_beside(3))
        encode(2 * c + 1)
        pl.when(jnp.logical_and(c == 1, first))(lambda: q_beside(2))
        place(c - 1, False)

        @pl.when(jnp.logical_and(c == C - 2, jnp.logical_not(first)))
        def _():
            for i in range(4, 8):
                q_paired(i)

        drain_units(2 * c - 2)
        drain_units(2 * c - 1)
        return carry

    lax.fori_loop(1, C, middle, 0)

    landed(str_.at[2 * C], "st", 2 * C, across)
    landed(trecv, "ts", 0, across)
    lined = ss[C, 0:TL, :] + str_[2 * C, TL : 2 * TL, :]
    factor = lax.rsqrt(as_column(lined) / D + epsilon) * 128 ** (-0.5)
    scaled = (town[...] + decoded(trecv[...], as_column(str_[2 * C, 0:TL, :]), 24)) * factor
    rounded = scaled.astype(jnp.bfloat16)
    low = e == 0
    qb[e] = jnp.where(low, rounded[:, :128], rounded[:, 128:])
    qs[...] = jnp.where(low, rounded[:, 128:], rounded[:, :128])
    token_query = rc(qs, qb.at[e], "q", 0, partner)
    token_query.start()

    def drain(c, carry):
        sent_chunk(c).wait_send()

        @pl.when(c < C - 1)
        def _():
            forward_copy(c).wait_send()
            pl.when(r < S - 1)(lambda: prior_copy(c, True).wait_send())

        pl.when(jnp.logical_and(r > 0, c < C - 2))(lambda: prior_forward(c).wait_send())
        return carry

    lax.fori_loop(0, C, drain, 0)
    drain_units(2 * C - 2)
    token_copy.wait_send()
    token_stat.wait_send()
    for i in range(8):
        ke(i).wait_send()
        qstep("qe", i, partner).wait_send()

    @pl.when(first)
    def _():
        for i in (0, 1, 2, 3, 7):
            kx(i).wait_send()
        for i in range(3):
            ky(i).wait_send()
        for i in range(8):
            kz(i).wait_send()
            qstep("qz", i, paired).wait_send()
        for i in range(4):
            qx(i).wait_send()
            qstep("qy", i, beside).wait_send()

    for copy in done:
        copy.wait_send()
    place(C - 1, True)
    drain_units(2 * C - 1)
    landed(qb.at[pe], "q", 0, partner)

    def settle(c, carry):
        landed(own_rows(pe, c), "fwd", c, partner)
        return carry

    lax.fori_loop(0, C, settle, 0)

    spans = half // SPAN

    def attend(those):
        scores = []
        for c in those:
            queries = qb[c // spans, rows(c % spans * SPAN, SPAN), :]
            keys = ctx[0, pl.ds(2 * c, 2)].reshape(NBR * RLEN, 128)
            scores.append(
                lax.dot_general(
                    queries, keys, (((1,), (1,)), ((), ())), preferred_element_type=f32
                )
            )
        raised = [jnp.exp(s - jnp.max(s, axis=1, keepdims=True)) for s in scores]
        weight = [(x / jnp.sum(x, axis=1, keepdims=True)).astype(jnp.bfloat16) for x in raised]
        for c, w in zip(those, weight):
            values = ctx[1, pl.ds(2 * c, 2)].reshape(NBR * RLEN, 128)
            mixed = jnp.dot(w, values, preferred_element_type=f32)
            out[rows(c * SPAN, SPAN), :] = mixed.astype(jnp.bfloat16)

    attend(range(1, 2 * spans))

    def settle_prior(c, carry):
        @pl.when(r > 0)
        def _():
            landed(ctx.at[:, pl.ds(0, 2), ctx_rows(pe, c), :], "pf", c, partner)

        return carry

    lax.fori_loop(0, C - 1, settle_prior, 0)

    @pl.when(r > 0)
    def _():
        landed(ctx.at[:, pl.ds(0, 2), ctx_rows(e, C - 1), :], "pr0", C - 1, below)
        across_core = {"seq": lax.rem(r + S - 1, S), "enc": pe}
        landed(ctx.at[:, pl.ds(0, 2), ctx_rows(pe, C - 1), :], "pr1", 0, across_core)

    attend([0])

    forward_copy(C - 1).wait_send()

    @pl.when(r < S - 1)
    def _():
        prior_copy(C - 1, True).wait_send()
        prior_copy(C - 1, False).wait_send()

    pl.when(r > 0)(lambda: prior_forward(C - 2).wait_send())
    token_query.wait_send()


def SEMAPHORES(S):
    C = CHUNKS
    return (
        ("kx", 8), ("ky", 3), ("kz", 8), ("ke", 8), ("wo", 2), ("qx", 4), ("qy", 4), ("qz", 8), ("qe", 8),
        ("x", C), ("t", 1), ("s", 2 * C), ("st", 2 * C + 1), ("ts", 1), ("tab", S), ("z", 2 * C * S),
        ("fwd", C), ("pr0", C), ("pr1", 1), ("pf", C), ("q", 1),
    )


def local_fused(tokens, nbr_feats, counts, slot_target, w_query, w_keyval):
    S = lax.axis_size("seq")
    cap = max(2, 2 * NB_SEQ // S)
    K = tokens.shape[1]
    half = tokens.shape[0] // 2
    C = CHUNKS
    bf, f32, i32 = jnp.bfloat16, jnp.float32, jnp.int32
    anywhere = pl.BlockSpec(memory_space=pl.ANY)
    vmem = pl.BlockSpec(memory_space=pltpu.VMEM)
    count = sum(size for _, size in SEMAPHORES(S))
    return pl.pallas_call(
        functools.partial(fused, S, cap),
        out_shape=jax.ShapeDtypeStruct((2 * half, 128), bf),
        in_specs=[vmem, vmem] + [anywhere] * 4,
        out_specs=vmem,
        scratch_shapes=[
            pltpu.VMEM((2, C, ENC_CAP, CROWS, K), bf),
            pltpu.VMEM((2, half, K), bf),
            pltpu.VMEM((2, 2 * K, 256), bf),
            pltpu.VMEM((2, 2 * K, 128), bf),
            pltpu.VMEM((2 * K, 256), bf),
            pltpu.VMEM((C, CFLAT, 256), f32),
            pltpu.VMEM((2 * C, KV_WORDS, 128), i32),
            pltpu.VMEM((2 * C, KV_WORDS, 128), i32),
            pltpu.VMEM((half, 256), f32),
            pltpu.VMEM((half * 3 // 4, 256), i32),
            pltpu.VMEM((half * 3 // 4, 256), i32),
            pltpu.VMEM((C + 1, 8, 128), f32),
            pltpu.VMEM((2 * C + 1, 8, 128), f32),
            pltpu.VMEM((2 * C + 1, 8, 128), f32),
            pltpu.VMEM((2 * C, ENC_CAP, CROWS, 128), bf),
            pltpu.VMEM((2 * C, S, cap, CROWS, 128), bf),
            pltpu.VMEM((C, 2, S, cap, CROWS, 128), bf),
            pltpu.VMEM((2, S * cap, CROWS, 128), bf),
            pltpu.VMEM((2, NB_SEQ + 2, RLEN, 128), bf),
            pltpu.VMEM((2, half, 128), bf),
            pltpu.VMEM((half, 128), bf),
            pltpu.VMEM((8, 128), i32),
            pltpu.VMEM((S, 8, 128), i32),
            pltpu.VMEM((8, 128), i32),
            pltpu.VMEM((8, 128), i32),
            pltpu.SMEM((8, 128), i32),
            pltpu.SMEM((8, 128), i32),
            pltpu.SemaphoreType.DMA((C + 5,)),
            pltpu.SemaphoreType.DMA((count,)),
            pltpu.SemaphoreType.DMA((count,)),
            pltpu.SemaphoreType.REGULAR((4,)),
        ],
        compiler_params=pltpu.CompilerParams(
            collective_id=0, has_side_effects=True, vmem_limit_bytes=56 << 20
        ),
    )(slot_target.reshape(1, -1), counts.reshape(1, -1), nbr_feats, tokens, w_query, w_keyval)


def solution(mesh):
    small = mesh.shape["mp"] == 2 and mesh.shape["groups"] == 2 and mesh.shape["seq"] == 4
    placed = (
        P(("groups", "seq"), ("mp", "enc")),
        P(("groups", "seq"), None, ("mp", "enc")),
        P("groups"),
        P(("groups", "seq")),
        P(None, ("mp", "enc")),
        P(None, ("mp", "enc")),
    )
    return jax.shard_map(
        local_fused if small else local,
        mesh=mesh,
        in_specs=placed,
        out_specs=P(("groups", "seq"), ("mp", "enc")),
        check_vma=False,
    )
```
